32 devices in a mesh: group: 2 (over x), expert: 16 (over z, y, core).
Axes of the slice: x: 2, y: 2, z: 4, core: 2. Of those that a mesh axis runs over, the one named last changes fastest.
Arguments:
- tokens: bfloat16 [64, 256, 1024], P(('group', 'expert')), parts along dimension 0, may hold values from -6 to 6
- w_qkv: bfloat16 [1024, 3072], P('expert'), may hold values from -0.1875 to 0.1875
- w_attn_out: bfloat16 [1024, 1024], P('expert'), may hold values from -0.1875 to 0.1875
- slot_keys: bfloat16 [1024, 32], replicated, may hold values from -0.5 to 0.5
- w_expert_in: bfloat16 [16, 1024, 2048], P('expert'), may hold values from -0.375 to 0.375
- w_expert_out: bfloat16 [16, 2048, 1024], P('expert'), may hold values from -0.125 to 0.125
Outputs:
- block_out: bfloat16 [64, 256, 1024], P(('group', 'expert')), parts along dimension 0
The draws below stay inside these ranges and needn't reach their ends.
There are 2 independent parts, one for each index of `group`. The reference program is written for one: setup_inputs(seed, part) draws one part's arguments, and reference() takes and returns one part's arrays. A program takes and returns all parts, laid end to end along the dimension named above; an argument that names none is the same for every part. Nothing has to cross between parts.
All inputs are finite; a program needn't handle non-finite values.
Results may differ from the reference program's by a relative error of at most 0.009.
Values may be sent and summed in bfloat16 or wider, within the bound.
No kernel may reach another device: no remote copies, remote signals or barrier semaphores. Data moves between devices by JAX's collectives and lax.ppermute only.
A program may use at most 64 MiB of HBM per device.

```python
import math
import jax
import jax.numpy as jnp
from jax import lax

D = 1024
HEADS = 16
HEAD_SIZE = 64
H = 2048
SEQ = 256
P_SIZE = 2
IMG_DEV = 2
EXPERTS = 16
SLOTS = 32
IMAGES = 32


def steps_of(own_key, extent, pieces, smallest, high):
    loudness = 1.0
    for axis_at, blocks in pieces:
        heights = jax.random.uniform(jax.random.fold_in(jax.random.fold_in(own_key, 6), axis_at), (blocks,), jnp.float32, smallest / len(pieces), high / len(pieces))
        loudness = loudness * jnp.repeat(jnp.exp(heights), extent[axis_at] // blocks).reshape((-1,) + (1,) * (len(extent) - 1 - axis_at))
    return loudness


def scatter_about(key, extent, scale, most, split=(), kind=jnp.bfloat16):
    result = scale * jax.random.normal(key, extent, jnp.float32)
    if split:
        result = result * steps_of(key, extent, split, -0.22, 0.18)
    return jnp.clip(result, -most, most).astype(kind)


def setup_inputs(seed: int = 0, part: int = 0) -> dict:
    splits = jax.random.split(jax.random.key(seed), 7)
    part_splits = jax.random.split(jax.random.fold_in(splits[6], part), 7)
    tokens = scatter_about(part_splits[0], (IMAGES, SEQ, D), 1.0, 6.0, ((0, 16),))
    w_qkv = scatter_about(splits[1], (D, 3 * D), D ** -0.5, 0.1875, ((0, 16),))
    w_attn_out = scatter_about(splits[2], (D, D), D ** -0.5, 0.1875, ((0, 16),))
    slot_keys = scatter_about(splits[3], (D, SLOTS), (D // 9) ** -0.5, 0.5)
    w_expert_in = scatter_about(splits[4], (EXPERTS, D, H), (D // 4) ** -0.5, 0.375, ((0, 16),))
    w_expert_out = scatter_about(splits[5], (EXPERTS, H, D), H ** -0.5, 0.125, ((0, 16),))
    return dict(tokens=tokens, w_qkv=w_qkv, w_attn_out=w_attn_out, slot_keys=slot_keys, w_expert_in=w_expert_in, w_expert_out=w_expert_out)


def layer_norm(values):
    center = values - lax.optimization_barrier(jnp.mean(values, axis=-1, keepdims=True))
    spread = lax.optimization_barrier(jnp.mean(center * center, axis=-1, keepdims=True))
    return center * lax.rsqrt(spread + 1e-06)

def attend_block(block, w_qkv, w_attn_out):
    count = block.shape[0]
    normed = layer_norm(block.astype(jnp.float32)).astype(jnp.bfloat16).reshape(count * SEQ, D)
    qkv = jnp.dot(normed, w_qkv, preferred_element_type=jnp.float32).astype(jnp.bfloat16)
    packed = qkv.reshape(count, SEQ, 3, HEADS, HEAD_SIZE)
    query = packed[:, :, 0].astype(jnp.float32)
    keys = packed[:, :, 1].astype(jnp.float32)
    values = packed[:, :, 2].astype(jnp.float32)
    scores = jnp.einsum('bqhd,bkhd->bhqk', query, keys) / math.sqrt(HEAD_SIZE)
    weights = jax.nn.softmax(scores, axis=-1).astype(jnp.bfloat16)
    attended = jnp.einsum('bhqk,bkhd->bqhd', weights.astype(jnp.float32), values).astype(jnp.bfloat16)
    attended = attended.reshape(count * SEQ, D)
    projected = jnp.dot(attended, w_attn_out, preferred_element_type=jnp.float32)
    return block.astype(jnp.float32) + projected.reshape(count, SEQ, D)

def reference(tokens, w_qkv, w_attn_out, slot_keys, w_expert_in, w_expert_out):
    blocks = tokens.reshape(IMAGES // IMG_DEV, IMG_DEV, SEQ, D)
    resid = lax.map(lambda block: attend_block(block, w_qkv, w_attn_out), blocks).reshape(IMAGES, SEQ, D)
    normed_two = layer_norm(resid).astype(jnp.bfloat16)
    logits = jnp.dot(normed_two.reshape(IMAGES * SEQ, D), slot_keys, preferred_element_type=jnp.float32)
    logits = logits.reshape(IMAGES, SEQ, SLOTS)
    dispatch = jax.nn.softmax(logits, axis=1).astype(jnp.bfloat16)
    combine = jax.nn.softmax(logits, axis=2).astype(jnp.bfloat16)
    slot_inputs = jnp.einsum('bsn,bsd->bnd', dispatch.astype(jnp.float32), normed_two.astype(jnp.float32)).astype(jnp.bfloat16)
    grouped = slot_inputs.reshape(IMAGES, EXPERTS, P_SIZE, D).transpose(1, 0, 2, 3).reshape(EXPERTS, IMAGES * P_SIZE, D)

    def one_expert(items):
        rows, first, second = items
        hidden = jax.nn.gelu(jnp.dot(rows, first, preferred_element_type=jnp.float32), approximate=False).astype(jnp.bfloat16)
        return jnp.dot(hidden, second, preferred_element_type=jnp.float32).astype(jnp.bfloat16)
    answered = lax.map(one_expert, (grouped, w_expert_in, w_expert_out))
    slot_outputs = answered.reshape(EXPERTS, IMAGES, P_SIZE, D).transpose(1, 0, 2, 3).reshape(IMAGES, SLOTS, D)
    mixed = jnp.einsum('bsn,bnd->bsd', combine.astype(jnp.float32), slot_outputs.astype(jnp.float32))
    return (resid + mixed).astype(jnp.bfloat16)
```

```python
import functools

import jax
import jax.numpy as jnp
from jax import lax
from jax.experimental import pallas as pl
from jax.experimental.pallas import tpu as pltpu
from jax.sharding import PartitionSpec as P

HEADS = 16
AXES = ("group", "expert")
F32 = jnp.float32
BF16 = jnp.bfloat16


def layer_norm(values):
    center = values - jnp.mean(values, axis=-1, keepdims=True)
    spread = jnp.mean(center * center, axis=-1, keepdims=True)
    return center * lax.rsqrt(spread + 1e-06)


def is_grid(groups, experts):
    return groups == 2 and experts == 16


def pairs_of(groups, experts, move):
    result = []
    for group in range(groups):
        mask, flip = move(group)
        for expert in range(experts):
            target = (group ^ flip) * experts + (expert ^ mask)
            result.append((group * experts + expert, target))
    return result


def gather_blocks(own, groups, experts):
    def send(block, move):
        return lax.ppermute(block, AXES, pairs_of(groups, experts, move))

    def over_y(block):
        return send(block, lambda group: (2, 0))

    def over_x(block):
        return send(block, lambda group: (0, 1))

    def in_chip(block):
        return send(block, lambda group: (1, 0))

    far = send(own, lambda group: (12, 0) if group else (8, 0))
    near = send(own, lambda group: (4, 0))
    beside = over_y(own)
    beside_near = over_y(near)
    far_other = over_x(far)
    beside_far = over_y(far)
    beside_far_other = over_x(beside_far)
    blocks = [
        (own, 0, 0),
        (beside, 2, 2),
        (near, 4, 4),
        (beside_near, 6, 6),
        (far, 8, 12),
        (far_other, 12, 8),
        (beside_far, 10, 14),
        (beside_far_other, 14, 10),
    ]
    return blocks + [(in_chip(b), m0 ^ 1, m1 ^ 1) for b, m0, m1 in blocks]


def gather_weight(own, mesh_shape):
    groups, experts = mesh_shape
    rows = own.shape[0]
    if not is_grid(groups, experts):
        return [lax.all_gather(own, "expert", axis=0, tiled=True)], jnp.zeros((1,), jnp.int32)
    blocks = gather_blocks(own, groups, experts)
    masks = jnp.array([[b[1] for b in blocks], [b[2] for b in blocks]], jnp.int32)
    mine = jnp.where(lax.axis_index("group") == 0, masks[0], masks[1])
    starts = jnp.bitwise_xor(mine, lax.axis_index("expert")) * rows
    return [b[0] for b in blocks], starts.astype(jnp.int32)


def load_pieces(starts_ref, pieces, whole, sem):
    copies = []
    for at, piece in enumerate(pieces):
        rows = piece.shape[0]
        start = pl.multiple_of(starts_ref[at], rows)
        copy = pltpu.make_async_copy(piece, whole.at[pl.ds(start, rows)], sem.at[at])
        copy.start()
        copies.append(copy)
    return copies


def attention_kernel(count, images, length, *refs):
    starts_ref, tokens_ref = refs[:2]
    pieces = refs[2 : 2 + count]
    out_ref = refs[2 + count]
    weight, normed, sem = refs[3 + count :]
    copies = load_pieces(starts_ref, pieces, weight, sem)
    width = tokens_ref.shape[1]
    for image in range(images):
        rows = slice(image * length, (image + 1) * length)
        normed[rows] = layer_norm(tokens_ref[rows].astype(F32)).astype(BF16)
    for copy in copies:
        copy.wait()
    head = width // HEADS
    pair = 2 * head
    group = 2 * pair
    scale = head**-0.5
    lane = lax.broadcasted_iota(jnp.int32, (length, pair), 1)
    first = lane < head

    def heads(at, carry):
        base = pl.multiple_of(at * group, group)

        def project(offset):
            return jnp.dot(
                normed[...], weight[:, pl.ds(base + offset, group)], preferred_element_type=F32
            )

        query = (project(0) * scale).astype(BF16)
        keys = project(width).astype(BF16)
        values = project(2 * width).astype(BF16)
        for image in range(images):
            rows = slice(image * length, (image + 1) * length)
            for half in range(2):
                columns = slice(half * pair, (half + 1) * pair)
                q, k, v = query[rows, columns], keys[rows, columns], values[rows, columns]
                result = []
                for mask in (first, ~first):
                    scores = lax.dot_general(
                        jnp.where(mask, q, jnp.zeros_like(q)),
                        k,
                        (((1,), (1,)), ((), ())),
                        preferred_element_type=F32,
                    )
                    top = jnp.max(scores, axis=-1, keepdims=True)
                    weights = jnp.exp(scores - top).astype(BF16)
                    mixed = jnp.dot(
                        weights, jnp.where(mask, v, jnp.ones_like(v)), preferred_element_type=F32
                    )
                    result.append(mixed / pltpu.roll(mixed, head, 1))
                out_ref[rows, pl.ds(base + half * pair, pair)] = jnp.where(
                    first, result[0], result[1]
                ).astype(BF16)
        return carry

    lax.fori_loop(0, width // group, heads, 0)


def attention(tokens, pieces, starts, images, length):
    rows, width = tokens.shape
    count = len(pieces)
    return pl.pallas_call(
        functools.partial(attention_kernel, count, images, length),
        out_shape=jax.ShapeDtypeStruct((rows, width), BF16),
        in_specs=[pl.BlockSpec(memory_space=pltpu.SMEM), pl.BlockSpec(memory_space=pltpu.VMEM)]
        + [pl.BlockSpec(memory_space=pl.ANY)] * count,
        out_specs=pl.BlockSpec(memory_space=pltpu.VMEM),
        scratch_shapes=[
            pltpu.VMEM((width, 3 * width), BF16),
            pltpu.VMEM((rows, width), BF16),
            pltpu.SemaphoreType.DMA((count,)),
        ],
        compiler_params=pltpu.CompilerParams(vmem_limit_bytes=40 << 20),
        cost_estimate=pl.CostEstimate(
            flops=2 * rows * width * (3 * width + 4 * length),
            bytes_accessed=6 * width * width + 4 * rows * width,
            transcendentals=rows * HEADS * length,
        ),
        name="attention",
    )(starts, tokens, *pieces)


def router_kernel(count, images, length, *refs):
    starts_ref, attended_ref, tokens_ref, keys_ref = refs[:4]
    pieces = refs[4 : 4 + count]
    resid_ref, combine_ref, inputs_ref = refs[4 + count : 7 + count]
    weight, sem = refs[7 + count :]
    for copy in load_pieces(starts_ref, pieces, weight, sem):
        copy.wait()
    for image in range(images):
        rows = slice(image * length, (image + 1) * length)
        resid = tokens_ref[rows].astype(F32) + jnp.dot(
            attended_ref[rows], weight[...], preferred_element_type=F32
        )
        resid_ref[rows] = resid
        normed = layer_norm(resid).astype(BF16)
        logits = lax.dot_general(
            keys_ref[...], normed, (((1,), (1,)), ((), ())), preferred_element_type=F32
        )
        dispatch = jax.nn.softmax(logits, axis=1).astype(BF16)
        combine_ref[image] = jax.nn.softmax(logits, axis=0).astype(BF16)
        inputs_ref[image] = jnp.dot(dispatch, normed, preferred_element_type=F32).astype(BF16)


def router(attended, tokens, slot_keys, pieces, starts, images, length):
    rows, width = tokens.shape
    slots = slot_keys.shape[1]
    count = len(pieces)
    vmem = pl.BlockSpec(memory_space=pltpu.VMEM)
    return pl.pallas_call(
        functools.partial(router_kernel, count, images, length),
        out_shape=[
            jax.ShapeDtypeStruct((rows, width), F32),
            jax.ShapeDtypeStruct((images, slots, length), BF16),
            jax.ShapeDtypeStruct((images, slots, width), BF16),
        ],
        in_specs=[pl.BlockSpec(memory_space=pltpu.SMEM)]
        + [vmem] * 3
        + [pl.BlockSpec(memory_space=pl.ANY)] * count,
        out_specs=[vmem] * 3,
        scratch_shapes=[
            pltpu.VMEM((width, width), BF16),
            pltpu.SemaphoreType.DMA((count,)),
        ],
        compiler_params=pltpu.CompilerParams(vmem_limit_bytes=40 << 20),
        cost_estimate=pl.CostEstimate(
            flops=2 * rows * width * (width + 2 * slots),
            bytes_accessed=2 * width * width + 8 * rows * width,
            transcendentals=2 * rows * slots,
        ),
        name="router",
    )(starts, attended, tokens, slot_keys.T, *pieces)


def on_device(mesh_shape, tokens, w_qkv, w_attn_out, slot_keys, w_expert_in, w_expert_out):
    images, length, width = tokens.shape
    flat_tokens = tokens.reshape(images * length, width)
    qkv_pieces, qkv_starts = gather_weight(w_qkv, mesh_shape)
    out_pieces, out_starts = gather_weight(w_attn_out, mesh_shape)
    attended = attention(flat_tokens, qkv_pieces, qkv_starts, images, length)
    resid, combine, slot_inputs = router(
        attended, flat_tokens, slot_keys, out_pieces, out_starts, images, length
    )
    slots = slot_keys.shape[1]
    sources = mesh_shape[1]
    expert_here = w_expert_in.shape[0]
    pairs = slots // (sources * expert_here)
    block = lax.all_to_all(slot_inputs, "expert", split_axis=1, concat_axis=1, tiled=True)
    arranged = block.reshape(images, sources, expert_here, pairs, width)
    hidden = jnp.einsum("bnepd,edh->bneph", arranged, w_expert_in, preferred_element_type=F32)
    hidden = jax.nn.gelu(hidden, approximate=False).astype(BF16)
    answer = jnp.einsum("bneph,ehd->bnepd", hidden, w_expert_out, preferred_element_type=F32)
    answered = answer.astype(BF16).reshape(images, slots, width)
    slot_outputs = lax.all_to_all(answered, "expert", split_axis=1, concat_axis=1, tiled=True)
    mixed = jnp.einsum("bns,bnd->bsd", combine, slot_outputs, preferred_element_type=F32)
    return (resid.reshape(images, length, width) + mixed).astype(BF16)


def solution(mesh):
    placed = (
        P(AXES, None, None),
        P("expert", None),
        P("expert", None),
        P(),
        P("expert", None, None),
        P("expert", None, None),
    )
    return jax.shard_map(
        functools.partial(on_device, (mesh.shape["group"], mesh.shape["expert"])),
        mesh=mesh,
        in_specs=placed,
        out_specs=P(AXES, None, None),
        check_vma=False,
    )
```

```python
import functools

import jax
import jax.numpy as jnp
from jax import lax
from jax.experimental import pallas as pl
from jax.experimental.pallas import tpu as pltpu
from jax.sharding import PartitionSpec as P

HEADS = 16
AXES = ("group", "expert")
F32 = jnp.float32
BF16 = jnp.bfloat16


def layer_norm(values):
    center = values - jnp.mean(values, axis=-1, keepdims=True)
    spread = jnp.mean(center * center, axis=-1, keepdims=True)
    return center * lax.rsqrt(spread + 1e-06)


def is_grid(groups, experts):
    return groups == 2 and experts == 16


def after(value, *earlier):
    return lax.optimization_barrier((value,) + earlier)[0]


def norm_kernel(tokens_ref, out_ref):
    out_ref[...] = layer_norm(tokens_ref[...].astype(F32)).astype(BF16)


def norm(tokens):
    rows, width = tokens.shape
    return pl.pallas_call(
        norm_kernel,
        out_shape=jax.ShapeDtypeStruct((rows, width), BF16),
        in_specs=[pl.BlockSpec(memory_space=pltpu.VMEM)],
        out_specs=pl.BlockSpec(memory_space=pltpu.VMEM),
        compiler_params=pltpu.CompilerParams(vmem_limit_bytes=16 << 20),
        cost_estimate=pl.CostEstimate(
            flops=8 * rows * width, bytes_accessed=4 * rows * width, transcendentals=rows
        ),
        name="norm",
    )(tokens)


def split_kernel(core_ref, qkv_ref, out_ref, keep_ref, give_ref):
    span = out_ref.shape[1] // 4
    for side, target in enumerate((keep_ref, give_ref)):
        core = jnp.bitwise_xor(core_ref[0], side)
        for chunk in range(2):
            for which in range(3):
                start = (which * 4 + core * 2 + chunk) * span
                at = (chunk * 3 + which) * span
                target[:, at : at + span] = qkv_ref[:, pl.ds(pl.multiple_of(start, span), span)]
        start = pl.multiple_of(core * 2 * span, 2 * span)
        target[:, 6 * span : 8 * span] = out_ref[:, pl.ds(start, 2 * span)]


def split(core, w_qkv, w_attn_out):
    rows, width = w_attn_out.shape
    vmem = pl.BlockSpec(memory_space=pltpu.VMEM)
    return pl.pallas_call(
        split_kernel,
        out_shape=[jax.ShapeDtypeStruct((rows, 2 * width), BF16)] * 2,
        in_specs=[pl.BlockSpec(memory_space=pltpu.SMEM), vmem, vmem],
        out_specs=[vmem] * 2,
        compiler_params=pltpu.CompilerParams(vmem_limit_bytes=8 << 20),
        cost_estimate=pl.CostEstimate(
            flops=0, bytes_accessed=16 * rows * width, transcendentals=0
        ),
        name="split",
    )(core.reshape(1), w_qkv, w_attn_out)


def load_blocks(place_ref, blocks, whole, sem, columns=slice(None)):
    core = place_ref[len(blocks)]
    half = blocks[0].shape[0] // 2
    copies = []
    for at, block in enumerate(blocks):
        for part in range(2):
            start = place_ref[at] * (2 * half) + jnp.bitwise_xor(core, part) * half
            copy = pltpu.make_async_copy(
                block.at[pl.ds(part * half, half)],
                whole.at[pl.ds(pl.multiple_of(start, half), half), columns],
                sem.at[2 * at + part],
            )
            copy.start()
            copies.append(copy)
    return copies


def attend(query, keys, values, head, out_ref, rows, columns):
    lane = lax.broadcasted_iota(jnp.int32, query.shape, 1)
    first = lane < head
    result = []
    for mask in (first, ~first):
        scores = lax.dot_general(
            jnp.where(mask, query, jnp.zeros_like(query)),
            keys,
            (((1,), (1,)), ((), ())),
            preferred_element_type=F32,
        )
        top = jnp.max(scores, axis=-1, keepdims=True)
        weights = jnp.exp(scores - top).astype(BF16)
        mixed = jnp.dot(
            weights, jnp.where(mask, values, jnp.ones_like(values)), preferred_element_type=F32
        )
        result.append(mixed / pltpu.roll(mixed, head, 1))
    out_ref[rows, columns] = jnp.where(first, result[0], result[1]).astype(BF16)


def attention_kernel(count, length, head, *refs):
    place_ref, mine_ref, other_ref = refs[:3]
    blocks = refs[3 : 3 + count]
    outs = refs[3 + count : 5 + count]
    weight, sem = refs[5 + count :]
    for copy in load_blocks(place_ref, blocks, weight, sem):
        copy.wait()
    span = weight.shape[1] // 3
    pair = 2 * head
    for normed, out_ref in zip((mine_ref, other_ref), outs):

        def project(at):
            return jnp.dot(
                normed[...], weight[:, at * span : (at + 1) * span], preferred_element_type=F32
            )

        query = (project(0) * head**-0.5).astype(BF16)
        keys = project(1).astype(BF16)
        values = project(2).astype(BF16)
        for start in range(0, normed.shape[0], length):
            rows = slice(start, start + length)
            for left in range(0, span, pair):
                columns = slice(left, left + pair)
                attend(
                    query[rows, columns],
                    keys[rows, columns],
                    values[rows, columns],
                    head,
                    out_ref,
                    rows,
                    columns,
                )


def attention(place, mine, other, blocks, length, head):
    rows, width = mine.shape
    count = len(blocks)
    span = blocks[0].shape[1] // 3
    vmem = pl.BlockSpec(memory_space=pltpu.VMEM)
    return pl.pallas_call(
        functools.partial(attention_kernel, count, length, head),
        out_shape=[jax.ShapeDtypeStruct((rows, span), BF16)] * 2,
        in_specs=[pl.BlockSpec(memory_space=pltpu.SMEM), vmem, vmem]
        + [pl.BlockSpec(memory_space=pltpu.HBM)] * count,
        out_specs=[vmem] * 2,
        scratch_shapes=[
            pltpu.VMEM((width, 3 * span), BF16),
            pltpu.SemaphoreType.DMA((2 * count,)),
        ],
        compiler_params=pltpu.CompilerParams(vmem_limit_bytes=24 << 20),
        cost_estimate=pl.CostEstimate(
            flops=4 * rows * span * (3 * width + 2 * length),
            bytes_accessed=6 * width * span + 4 * rows * width,
            transcendentals=2 * rows * (span // head) * length,
        ),
        name="attention",
    )(place, mine, other, *blocks)


def router_kernel(count, images, length, *refs):
    place_ref, tokens_ref, keys_ref = refs[:3]
    parts = refs[3:7]
    blocks = refs[7 : 7 + 2 * count]
    resid_ref, combine_ref, inputs_ref = refs[7 + 2 * count : 10 + 2 * count]
    weight, sem = refs[10 + 2 * count :]
    core = place_ref[count]
    span = blocks[0].shape[1]
    copies = []
    for side in range(2):
        left = pl.multiple_of(jnp.bitwise_xor(core, side) * span, span)
        copies += load_halves(
            place_ref, blocks[side * count : (side + 1) * count], weight, sem, left, span, core, side
        )
    for copy in copies:
        copy.wait()
    inner = parts[0].shape[1]
    for image in range(images):
        at = slice(image * length, (image + 1) * length)
        resid = tokens_ref[at].astype(F32)
        for which, part in enumerate(parts):
            side, chunk = which // 2, which % 2
            start = (2 * jnp.bitwise_xor(core, side) + chunk) * inner
            resid += jnp.dot(
                part[at],
                weight[pl.ds(pl.multiple_of(start, inner), inner)],
                preferred_element_type=F32,
            )
        resid_ref[at] = resid
        normed = layer_norm(resid).astype(BF16)
        logits = lax.dot_general(
            keys_ref[...], normed, (((1,), (1,)), ((), ())), preferred_element_type=F32
        )
        dispatch = jax.nn.softmax(logits, axis=1).astype(BF16)
        combine_ref[image] = jax.nn.softmax(logits, axis=0).astype(BF16)
        inputs_ref[image] = jnp.dot(dispatch, normed, preferred_element_type=F32).astype(BF16)


def load_halves(place_ref, blocks, whole, sem, left, span, core, side):
    half = blocks[0].shape[0] // 2
    copies = []
    for at, block in enumerate(blocks):
        for part in range(2):
            start = place_ref[at] * (2 * half) + jnp.bitwise_xor(core, part ^ side) * half
            copy = pltpu.make_async_copy(
                block.at[pl.ds(part * half, half)],
                whole.at[pl.ds(pl.multiple_of(start, half), half), pl.ds(left, span)],
                sem.at[(side * len(blocks) + at) * 2 + part],
            )
            copy.start()
            copies.append(copy)
    return copies


def router(place, tokens, slot_keys, parts, blocks, images, length):
    rows, width = tokens.shape
    slots = slot_keys.shape[1]
    count = place.shape[0] - 1
    vmem = pl.BlockSpec(memory_space=pltpu.VMEM)
    hbm = pl.BlockSpec(memory_space=pltpu.HBM)
    return pl.pallas_call(
        functools.partial(router_kernel, count, images, length),
        out_shape=[
            jax.ShapeDtypeStruct((rows, width), F32),
            jax.ShapeDtypeStruct((images, slots, length), BF16),
            jax.ShapeDtypeStruct((images, slots, width), BF16),
        ],
        in_specs=[pl.BlockSpec(memory_space=pltpu.SMEM)] + [vmem] * 6 + [hbm] * 2 * count,
        out_specs=[vmem] * 3,
        scratch_shapes=[
            pltpu.VMEM((width, width), BF16),
            pltpu.SemaphoreType.DMA((4 * count,)),
        ],
        compiler_params=pltpu.CompilerParams(vmem_limit_bytes=24 << 20),
        cost_estimate=pl.CostEstimate(
            flops=2 * rows * width * (width + 2 * slots),
            bytes_accessed=2 * width * width + 8 * rows * width,
            transcendentals=2 * rows * slots,
        ),
        name="router",
    )(place, tokens, slot_keys.T, *parts, *blocks)


def front_on_grid(groups, experts, tokens, w_qkv, w_attn_out, slot_keys):
    images, length, width = tokens.shape
    head = width // HEADS
    flat = tokens.reshape(images * length, width)
    expert = lax.axis_index("expert")
    group = lax.axis_index("group")
    core = expert % 2
    rows = w_qkv.shape[0]

    def send(value, move):
        pairs = []
        for at in range(groups):
            mask, flip = move(at)
            for index in range(experts):
                target = (at ^ flip) * experts + (index ^ mask)
                pairs.append((at * experts + index, target))
        return lax.ppermute(value, AXES, pairs)

    def in_chip(value):
        return send(value, lambda at: (1, 0))

    def over_y(value):
        return send(value, lambda at: (2, 0))

    def near_z(value):
        return send(value, lambda at: (4, 0))

    def far_z(value):
        return send(value, lambda at: (12, 0) if at else (8, 0))

    def over_x(value):
        return send(value, lambda at: (0, 1))

    span = width // 4
    keep, give = split(core, w_qkv, w_attn_out)
    block = jnp.concatenate([keep, in_chip(give)], axis=0)
    a = block[:, : 3 * span]
    b = block[:, 3 * span : 6 * span]
    c = block[:, 6 * span :]

    c_far = far_z(c)
    c_near = near_z(c)
    c_y = over_y(c)
    a_far = far_z(a)
    a_y = over_y(a)
    a_near = near_z(after(a, c_y))
    c_y_far = over_y(after(c_far, c_y))
    c_x = over_x(after(c_far, c_y))
    c_y_near = over_y(after(c_near, a_y))
    b_y = over_y(after(b, c_y_far, c_x))
    b_far = far_z(after(b, c_y_far, c_x))
    c_x_far = over_x(c_y_far)
    a_y_far = over_y(after(a_far, c_y_near))
    a_x = over_x(after(a_far, c_y_near))
    a_y_near = over_y(after(a_near, b_y))
    b_near = near_z(after(b, a_near, a_x))
    normed = norm(after(flat, a_x))
    normed_other = in_chip(normed)
    a_x_far = over_x(a_y_far)
    b_y_far = over_y(after(b_far, a_y_near))
    b_x = over_x(after(b_far, a_y_near))
    b_y_near = over_y(after(b_near, a_x_far))
    b_x_far = over_x(b_y_far)

    a_blocks = [a, a_y, a_near, a_y_near, a_far, a_x, a_y_far, a_x_far]
    b_blocks = [b, b_y, b_near, b_y_near, b_far, b_x, b_y_far, b_x_far]
    c_blocks = [c, c_y, c_near, c_y_near, c_far, c_x, c_y_far, c_x_far]
    masks = jnp.array([[0, 1, 2, 3, 4, 6, 5, 7, 0], [0, 1, 2, 3, 6, 4, 7, 5, 0]], jnp.int32)
    chips = jnp.bitwise_xor(jnp.where(group == 0, masks[0], masks[1]), expert // 2)
    last = lax.broadcasted_iota(jnp.int32, chips.shape, 0) == len(a_blocks)
    place = jnp.where(last, core, chips).astype(jnp.int32)

    mine_a, other_a = attention(
        place, after(normed, b_y_far, b_x), normed_other, a_blocks, length, head
    )
    mine_b, other_b = attention(place, normed, after(normed_other, mine_a), b_blocks, length, head)
    c_blocks += [in_chip(after(block, a_far)) for block in c_blocks[:5]] + [
        in_chip(after(block, a_x)) for block in c_blocks[5:]
    ]
    parts = [mine_a, mine_b, in_chip(other_a), in_chip(other_b)]
    return router(place, flat, slot_keys, parts, c_blocks, images, length)


def front(tokens, w_qkv, w_attn_out, slot_keys):
    images, length, width = tokens.shape
    head = width // HEADS
    rows = images * length
    normed = layer_norm(tokens.astype(F32)).astype(BF16).reshape(rows, width)
    full_qkv = lax.all_gather(w_qkv, "expert", axis=0, tiled=True)
    qkv = jnp.dot(normed, full_qkv, preferred_element_type=F32).astype(BF16)
    query, keys, values = [
        part[:, :, 0] for part in jnp.split(qkv.reshape(images, length, 3, HEADS, head), 3, axis=2)
    ]
    scores = jnp.einsum("bqhd,bkhd->bhqk", query, keys, preferred_element_type=F32) * head**-0.5
    weights = jax.nn.softmax(scores, axis=-1).astype(BF16)
    attended = jnp.einsum("bhqk,bkhd->bqhd", weights, values, preferred_element_type=F32)
    full_out = lax.all_gather(w_attn_out, "expert", axis=0, tiled=True)
    projected = jnp.dot(
        attended.astype(BF16).reshape(rows, width), full_out, preferred_element_type=F32
    )
    resid = tokens.astype(F32).reshape(rows, width) + projected
    normed_two = layer_norm(resid).astype(BF16).reshape(images, length, width)
    logits = jnp.einsum("bsd,dn->bns", normed_two, slot_keys, preferred_element_type=F32)
    dispatch = jax.nn.softmax(logits, axis=2).astype(BF16)
    combine = jax.nn.softmax(logits, axis=1).astype(BF16)
    slot_inputs = jnp.einsum("bns,bsd->bnd", dispatch, normed_two, preferred_element_type=F32)
    return resid, combine, slot_inputs.astype(BF16)


def on_device(mesh_shape, tokens, w_qkv, w_attn_out, slot_keys, w_expert_in, w_expert_out):
    images, length, width = tokens.shape
    if is_grid(*mesh_shape):
        resid, combine, slot_inputs = front_on_grid(
            *mesh_shape, tokens, w_qkv, w_attn_out, slot_keys
        )
    else:
        resid, combine, slot_inputs = front(tokens, w_qkv, w_attn_out, slot_keys)
    slots = slot_keys.shape[1]
    sources = mesh_shape[1]
    expert_here = w_expert_in.shape[0]
    pairs = slots // (sources * expert_here)
    block = lax.all_to_all(slot_inputs, "expert", split_axis=1, concat_axis=1, tiled=True)
    arranged = block.reshape(images, sources, expert_here, pairs, width)
    hidden = jnp.einsum("bnepd,edh->bneph", arranged, w_expert_in, preferred_element_type=F32)
    hidden = jax.nn.gelu(hidden, approximate=False).astype(BF16)
    answer = jnp.einsum("bneph,ehd->bnepd", hidden, w_expert_out, preferred_element_type=F32)
    answered = answer.astype(BF16).reshape(images, slots, width)
    slot_outputs = lax.all_to_all(answered, "expert", split_axis=1, concat_axis=1, tiled=True)
    mixed = jnp.einsum("bns,bnd->bsd", combine, slot_outputs, preferred_element_type=F32)
    return (resid.reshape(images, length, width) + mixed).astype(BF16)


def solution(mesh):
    placed = (
        P(AXES, None, None),
        P("expert", None),
        P("expert", None),
        P(),
        P("expert", None, None),
        P("expert", None, None),
    )
    return jax.shard_map(
        functools.partial(on_device, (mesh.shape["group"], mesh.shape["expert"])),
        mesh=mesh,
        in_specs=placed,
        out_specs=P(AXES, None, None),
        check_vma=False,
    )
```

```python
import functools

import jax
import jax.numpy as jnp
from jax import lax
from jax.experimental import pallas as pl
from jax.experimental.pallas import tpu as pltpu
from jax.sharding import PartitionSpec as P

HEADS = 16
EXPERT_STEPS = 4
CHIPS = 8
LONG = 1 << 34
EARLY = (0, 1, 2, 4, 6)
LATE = (3, 5, 7)
AXES = ("group", "expert")
F32 = jnp.float32
BF16 = jnp.bfloat16


def layer_norm(values):
    center = values - jnp.mean(values, axis=-1, keepdims=True)
    spread = jnp.mean(center * center, axis=-1, keepdims=True)
    return center * lax.rsqrt(spread + 1e-06)


def is_grid(groups, experts):
    return groups == 2 and experts == 16


def chip_of(block):
    far = lax.axis_index("group") * 2
    mask = (block, block, block, block, 4 + far, 6 - far, 5 + far, 7 - far)[block]
    return jnp.bitwise_xor(lax.axis_index("expert") // 2, mask)


def core_of():
    return lax.axis_index("expert") % 2


def norm_kernel(tokens_ref, *refs):
    mine_ref, other_ref, scratch = refs[-3:]
    scratch[...] = layer_norm(tokens_ref[...].astype(F32)).astype(BF16)
    core = core_of()
    block = mine_ref.shape[1] // CHIPS
    for at in range(CHIPS):
        start = pl.multiple_of(chip_of(at) * block, block)
        columns = scratch[:, pl.ds(start, block)]
        swapped = pltpu.roll(columns.astype(F32), block // 2, 1).astype(BF16)
        place = slice(at * block, (at + 1) * block)
        mine_ref[:, place] = jnp.where(core == 0, columns, swapped)
        other_ref[:, place] = jnp.where(core == 0, swapped, columns)


def norm(tokens, image, length, before, others=(), cost=0):
    rows, width = tokens.shape
    piece = pl.BlockSpec((length, width), lambda step: (image, 0))
    return pl.pallas_call(
        norm_kernel,
        out_shape=[jax.ShapeDtypeStruct((rows, width), BF16)] * 2,
        grid=(1,),
        in_specs=[piece] + [pl.BlockSpec(memory_space=pl.ANY)] * len((*others, *before)),
        out_specs=[piece] * 2,
        scratch_shapes=[pltpu.VMEM((length, width), BF16)],
        input_output_aliases={1: 0, 2: 1} if others else {},
        compiler_params=pltpu.CompilerParams(vmem_limit_bytes=16 << 20),
        cost_estimate=pl.CostEstimate(
            flops=cost or 8 * length * width,
            bytes_accessed=6 * length * width,
            transcendentals=length,
        ),
        name="norm",
    )(tokens, *others, *before)


def copy_kernel(count, *refs):
    for source, target in zip(refs[:count], refs[-count:]):
        target[...] = source[...]


def copies(values, before):
    vmem = pl.BlockSpec(memory_space=pltpu.VMEM)
    return pl.pallas_call(
        functools.partial(copy_kernel, len(values)),
        out_shape=[jax.ShapeDtypeStruct(value.shape, value.dtype) for value in values],
        in_specs=[vmem] * len(values) + [pl.BlockSpec(memory_space=pl.ANY)] * len(before),
        out_specs=[vmem] * len(values),
        compiler_params=pltpu.CompilerParams(vmem_limit_bytes=4 << 20),
        cost_estimate=pl.CostEstimate(flops=0, bytes_accessed=0, transcendentals=0),
        name="copies",
    )(*values, *before)


def split_kernel(weight_ref, *refs):
    span = weight_ref.shape[1] // 12
    for side, target in enumerate(refs[-2:]):
        core = jnp.bitwise_xor(core_of(), side)
        for chunk in range(2):
            for which in range(3):
                start = (which * 4 + core * 2 + chunk) * span
                at = (chunk * 3 + which) * span
                target[:, at : at + span] = weight_ref[:, pl.ds(pl.multiple_of(start, span), span)]


def split_out_kernel(weight_ref, *refs):
    span = weight_ref.shape[1] // 2
    for side, target in enumerate(refs[-2:]):
        start = jnp.bitwise_xor(core_of(), side) * span
        target[...] = weight_ref[:, pl.ds(pl.multiple_of(start, span), span)]


def split(kernel, weight, before=()):
    rows, columns = weight.shape
    vmem = pl.BlockSpec(memory_space=pltpu.VMEM)
    return pl.pallas_call(
        kernel,
        out_shape=[jax.ShapeDtypeStruct((rows, columns // 2), BF16)] * 2,
        in_specs=[vmem] + [pl.BlockSpec(memory_space=pl.ANY)] * len(before),
        out_specs=[vmem] * 2,
        compiler_params=pltpu.CompilerParams(vmem_limit_bytes=8 << 20),
        cost_estimate=pl.CostEstimate(
            flops=0, bytes_accessed=4 * rows * columns, transcendentals=0
        ),
        name="split",
    )(weight, *before)


def attend(query, keys, values, head, out_ref, rows, columns):
    lane = lax.broadcasted_iota(jnp.int32, query.shape, 1)
    first = lane < head
    result = []
    for mask in (first, ~first):
        scores = lax.dot_general(
            jnp.where(mask, query, jnp.zeros_like(query)),
            keys,
            (((1,), (1,)), ((), ())),
            preferred_element_type=F32,
        )
        top = jnp.max(scores, axis=-1, keepdims=True)
        weights = jnp.exp(scores - top).astype(BF16)
        mixed = jnp.dot(
            weights, jnp.where(mask, values, jnp.ones_like(values)), preferred_element_type=F32
        )
        result.append(mixed / pltpu.roll(mixed, head, 1))
    out_ref[rows, columns] = jnp.where(first, result[0], result[1]).astype(BF16)


def attention_kernel(length, head, normed, weight, *refs):
    out_ref = refs[-1]
    span = out_ref.shape[1]
    pair = 2 * head

    def project(at):
        return jnp.dot(
            normed[...], weight[:, at * span : (at + 1) * span], preferred_element_type=F32
        )

    query = (project(0) * head**-0.5).astype(BF16)
    keys = project(1).astype(BF16)
    values = project(2).astype(BF16)
    for start in range(0, normed.shape[0], length):
        rows = slice(start, start + length)
        for left in range(0, span, pair):
            columns = slice(left, left + pair)
            attend(
                query[rows, columns],
                keys[rows, columns],
                values[rows, columns],
                head,
                out_ref,
                rows,
                columns,
            )


def attention(normed, weight, length, head, before=()):
    rows, width = normed.shape
    span = weight.shape[1] // 3
    vmem = pl.BlockSpec(memory_space=pltpu.VMEM)
    return pl.pallas_call(
        functools.partial(attention_kernel, length, head),
        out_shape=jax.ShapeDtypeStruct((rows, span), BF16),
        in_specs=[vmem] * 2 + [pl.BlockSpec(memory_space=pl.ANY)] * len(before),
        out_specs=vmem,
        compiler_params=pltpu.CompilerParams(vmem_limit_bytes=20 << 20),
        cost_estimate=pl.CostEstimate(
            flops=2 * rows * span * (3 * width + 2 * length),
            bytes_accessed=6 * width * span + 4 * rows * width,
            transcendentals=rows * (span // head) * length,
        ),
        name="attention",
    )(normed, weight, *before)


def router_kernel(count, images, length, *refs):
    tokens_ref, keys_ref = refs[:2]
    parts = refs[2:6]
    sources = refs[6:10]
    resid_ref, combine_ref, inputs_ref = refs[10:13]
    weight, sem = refs[13:]
    core = core_of()
    span = sources[0].shape[1]
    half = weight.shape[0] // (2 * count)
    copies = []
    for which, source in enumerate(sources):
        side = which // 2
        left = pl.multiple_of(jnp.bitwise_xor(core, side) * span, span)
        for at, block in enumerate((EARLY, LATE)[which % 2]):
            for part in range(2):
                start = (2 * chip_of(block) + jnp.bitwise_xor(core, part ^ side)) * half
                copy = pltpu.make_async_copy(
                    source.at[pl.ds((2 * at + part) * half, half)],
                    weight.at[pl.ds(pl.multiple_of(start, half), half), pl.ds(left, span)],
                    sem.at[len(copies)],
                )
                copy.start()
                copies.append(copy)
    for copy in copies:
        copy.wait()
    inner = parts[0].shape[1]
    for image in range(images):
        at = slice(image * length, (image + 1) * length)
        resid = tokens_ref[at].astype(F32)
        for which, part in enumerate(parts):
            side, chunk = which // 2, which % 2
            start = (2 * jnp.bitwise_xor(core, side) + chunk) * inner
            resid += jnp.dot(
                part[at],
                weight[pl.ds(pl.multiple_of(start, inner), inner)],
                preferred_element_type=F32,
            )
        resid_ref[at] = resid
        normed = layer_norm(resid).astype(BF16)
        logits = lax.dot_general(
            keys_ref[...], normed, (((1,), (1,)), ((), ())), preferred_element_type=F32
        )
        dispatch = jax.nn.softmax(logits, axis=1).astype(BF16)
        combine_ref[image] = jax.nn.softmax(logits, axis=0).astype(BF16)
        inputs_ref[image] = jnp.dot(dispatch, normed, preferred_element_type=F32).astype(BF16)


def router(tokens, slot_keys, parts, blocks, images, length):
    rows, width = tokens.shape
    slots = slot_keys.shape[1]
    count = CHIPS
    vmem = pl.BlockSpec(memory_space=pltpu.VMEM)
    hbm = pl.BlockSpec(memory_space=pl.ANY)
    return pl.pallas_call(
        functools.partial(router_kernel, count, images, length),
        out_shape=[
            jax.ShapeDtypeStruct((rows, width), F32),
            jax.ShapeDtypeStruct((images, slots, length), BF16),
            jax.ShapeDtypeStruct((images, slots, width), BF16),
        ],
        in_specs=[vmem] * 6 + [hbm] * 4,
        out_specs=[vmem] * 3,
        scratch_shapes=[
            pltpu.VMEM((width, width), BF16),
            pltpu.SemaphoreType.DMA((4 * count,)),
        ],
        compiler_params=pltpu.CompilerParams(vmem_limit_bytes=24 << 20),
        cost_estimate=pl.CostEstimate(
            flops=2 * rows * width * (width + 2 * slots),
            bytes_accessed=2 * width * width + 8 * rows * width,
            transcendentals=2 * rows * slots,
        ),
        name="router",
    )(tokens, slot_keys.T, *parts, *blocks)


def expert_kernel(inputs_ref, first_ref, second_ref, out_ref, total):
    step = pl.program_id(1)
    hidden = jnp.dot(inputs_ref[0], first_ref[0], preferred_element_type=F32)
    hidden = (0.5 * hidden * (1.0 + lax.erf(hidden * 0.5**0.5))).astype(BF16)
    answer = jnp.dot(hidden, second_ref[0], preferred_element_type=F32)

    @pl.when(step == 0)
    def _():
        total[...] = answer

    @pl.when(step > 0)
    def _():
        total[...] += answer

    @pl.when(step == pl.num_programs(1) - 1)
    def _():
        out_ref[0] = total[...].astype(BF16)


def experts_here(inputs, first, second):
    count, rows, width = inputs.shape
    hidden = first.shape[2]
    piece = hidden // EXPERT_STEPS
    return pl.pallas_call(
        expert_kernel,
        out_shape=jax.ShapeDtypeStruct(inputs.shape, BF16),
        grid=(count, EXPERT_STEPS),
        in_specs=[
            pl.BlockSpec((1, rows, width), lambda e, h: (e, 0, 0)),
            pl.BlockSpec((1, width, piece), lambda e, h: (e, 0, h)),
            pl.BlockSpec((1, piece, width), lambda e, h: (e, h, 0)),
        ],
        out_specs=pl.BlockSpec((1, rows, width), lambda e, h: (e, 0, 0)),
        scratch_shapes=[pltpu.VMEM((rows, width), F32)],
        compiler_params=pltpu.CompilerParams(vmem_limit_bytes=24 << 20),
        cost_estimate=pl.CostEstimate(
            flops=4 * count * rows * width * hidden,
            bytes_accessed=4 * count * width * hidden,
            transcendentals=count * rows * hidden,
        ),
        name="experts",
    )(inputs, first, second)


def front_on_grid(groups, experts, tokens, w_qkv, w_attn_out, slot_keys):
    images, length, width = tokens.shape
    head = width // HEADS
    flat = tokens.reshape(images * length, width)
    def send(value, move):
        pairs = []
        for at in range(groups):
            mask, flip = move(at)
            for index in range(experts):
                target = (at ^ flip) * experts + (index ^ mask)
                pairs.append((at * experts + index, target))
        return lax.ppermute(value, AXES, pairs)

    def in_chip(value):
        return send(value, lambda at: (1, 0))

    def over_y(value):
        return send(value, lambda at: (2, 0))

    def near_z(value):
        return send(value, lambda at: (4, 0))

    def far_z(value):
        return send(value, lambda at: (12, 0) if at else (8, 0))

    def over_x(value):
        return send(value, lambda at: (0, 1))

    span = width // 4
    keep, give = split(split_kernel, w_qkv)
    block = jnp.concatenate([keep, in_chip(give)], axis=0)
    a = block[:, : 3 * span]
    b = block[:, 3 * span :]

    def whole(*blocks):
        return jnp.concatenate(blocks, axis=0)

    def step(*values, done=()):
        nonlocal token
        *result, token = copies([*values, token], done)
        return result

    a_far = far_z(a)
    a_near = near_z(a)
    a_y = over_y(a)
    normed, normed_sent = norm(flat, 0, length, (a,), cost=LONG)
    token = normed[:8, :128]
    (b_1,) = step(b)
    b_y = over_y(b_1)
    a_far_1, b_2 = step(a_far, b, done=(a_y, a_near))
    b_far = far_z(b_2)
    a_x = over_x(a_far_1)
    a_y_far = over_y(a_far_1)
    (a_near_1,) = step(a_near, done=(b_y,))
    a_y_near = over_y(a_near_1)
    for image in range(1, images):
        normed, normed_sent = norm(flat, image, length, (token,), (normed, normed_sent), LONG)
    (a_y_far_1,) = step(a_y_far)
    a_x_far = over_x(a_y_far_1)
    out_keep, out_give = split(split_out_kernel, w_attn_out, (token,))
    c = jnp.concatenate([out_keep, in_chip(out_give)], axis=0)
    b_3, c_1 = step(b, c, done=(a_x,))
    b_near = near_z(b_3)
    c_y = over_y(c_1)
    normed_other = in_chip(normed_sent)
    b_far_1, c_2 = step(b_far, c, done=(a_y_near, a_x_far))
    b_x = over_x(b_far_1)
    b_y_far = over_y(b_far_1)
    c_far = far_z(c_2)
    a_all = whole(a, a_y, a_near, a_y_near, a_far, a_x, a_y_far, a_x_far)
    other_a = attention(normed_other, a_all, length, head, (token,))
    mine_a = attention(normed, a_all, length, head, (other_a,))
    (b_near_1,) = step(b_near, done=(mine_a, c_y))
    b_y_near = over_y(b_near_1)
    (b_y_far_1,) = step(b_y_far)
    b_x_far = over_x(b_y_far_1)
    (c_3,) = step(c, done=(b_x,))
    c_near = near_z(c_3)
    (c_far_1,) = step(c_far)
    c_y_far = over_y(c_far_1)
    c_x = over_x(c_far_1)
    (c_near_1,) = step(c_near, done=(b_y_near,))
    c_y_near = over_y(c_near_1)
    (c_y_far_1,) = step(c_y_far)
    c_x_far = over_x(c_y_far_1)
    (other_a_1,) = step(other_a, done=(b_x_far,))
    parts_a = in_chip(other_a_1)
    b_all = whole(b, b_y, b_near, b_y_near, b_far, b_x, b_y_far, b_x_far)
    other_b = attention(normed_other, b_all, length, head, (token,))
    early = whole(c, c_y, c_near, c_far, c_y_far)
    late = whole(*step(c_y_near, c_x, c_x_far, done=(other_b,)))
    parts_b = in_chip(other_b)
    mine_b = attention(normed, b_all, length, head, (other_b,))
    parts = [mine_a, mine_b, parts_a, parts_b]
    outs = [early, late, in_chip(early), in_chip(late)]
    return router(flat, slot_keys, parts, outs, images, length)


def front(tokens, w_qkv, w_attn_out, slot_keys):
    images, length, width = tokens.shape
    head = width // HEADS
    rows = images * length
    normed = layer_norm(tokens.astype(F32)).astype(BF16).reshape(rows, width)
    full_qkv = lax.all_gather(w_qkv, "expert", axis=0, tiled=True)
    qkv = jnp.dot(normed, full_qkv, preferred_element_type=F32).astype(BF16)
    query, keys, values = [
        part[:, :, 0] for part in jnp.split(qkv.reshape(images, length, 3, HEADS, head), 3, axis=2)
    ]
    scores = jnp.einsum("bqhd,bkhd->bhqk", query, keys, preferred_element_type=F32) * head**-0.5
    weights = jax.nn.softmax(scores, axis=-1).astype(BF16)
    attended = jnp.einsum("bhqk,bkhd->bqhd", weights, values, preferred_element_type=F32)
    full_out = lax.all_gather(w_attn_out, "expert", axis=0, tiled=True)
    projected = jnp.dot(
        attended.astype(BF16).reshape(rows, width), full_out, preferred_element_type=F32
    )
    resid = tokens.astype(F32).reshape(rows, width) + projected
    normed_two = layer_norm(resid).astype(BF16).reshape(images, length, width)
    logits = jnp.einsum("bsd,dn->bns", normed_two, slot_keys, preferred_element_type=F32)
    dispatch = jax.nn.softmax(logits, axis=2).astype(BF16)
    combine = jax.nn.softmax(logits, axis=1).astype(BF16)
    slot_inputs = jnp.einsum("bns,bsd->bnd", dispatch, normed_two, preferred_element_type=F32)
    return resid, combine, slot_inputs.astype(BF16)


def on_device(mesh_shape, tokens, w_qkv, w_attn_out, slot_keys, w_expert_in, w_expert_out):
    images, length, width = tokens.shape
    if is_grid(*mesh_shape):
        resid, combine, slot_inputs = front_on_grid(
            *mesh_shape, tokens, w_qkv, w_attn_out, slot_keys
        )
    else:
        resid, combine, slot_inputs = front(tokens, w_qkv, w_attn_out, slot_keys)
    slots = slot_keys.shape[1]
    sources = mesh_shape[1]
    expert_here = w_expert_in.shape[0]
    pairs = slots // (sources * expert_here)
    block = lax.all_to_all(slot_inputs, "expert", split_axis=1, concat_axis=1, tiled=True)
    arranged = block.reshape(images, sources, expert_here, pairs, width)
    arranged = arranged.transpose(2, 0, 1, 3, 4).reshape(expert_here, -1, width)
    answer = experts_here(arranged, w_expert_in, w_expert_out)
    answer = answer.reshape(expert_here, images, sources, pairs, width)
    answered = answer.transpose(1, 2, 0, 3, 4).reshape(images, slots, width)
    slot_outputs = lax.all_to_all(answered, "expert", split_axis=1, concat_axis=1, tiled=True)
    mixed = jnp.einsum("bns,bnd->bsd", combine, slot_outputs, preferred_element_type=F32)
    return (resid.reshape(images, length, width) + mixed).astype(BF16)


def solution(mesh):
    placed = (
        P(AXES, None, None),
        P("expert", None),
        P("expert", None),
        P(),
        P("expert", None, None),
        P("expert", None, None),
    )
    return jax.shard_map(
        functools.partial(on_device, (mesh.shape["group"], mesh.shape["expert"])),
        mesh=mesh,
        in_specs=placed,
        out_specs=P(AXES, None, None),
        check_vma=False,
    )
```

```python
import functools

import jax
import jax.numpy as jnp
from jax import lax
from jax.experimental import pallas as pl
from jax.experimental.pallas import tpu as pltpu
from jax.sharding import PartitionSpec as P

HEADS = 16
EXPERT_STEPS = 2
CHIPS = 8
LONG = 1 << 34
EARLY = (0, 1, 2, 4, 6)
LATE = (3, 5, 7)
AXES = ("group", "expert")
F32 = jnp.float32
BF16 = jnp.bfloat16


def layer_norm(values):
    center = values - jnp.mean(values, axis=-1, keepdims=True)
    spread = jnp.mean(center * center, axis=-1, keepdims=True)
    return center * lax.rsqrt(spread + 1e-06)


def is_grid(groups, experts):
    return groups == 2 and experts == 16


def chip_of(block):
    far = lax.axis_index("group") * 2
    mask = (block, block, block, block, 4 + far, 6 - far, 5 + far, 7 - far)[block]
    return jnp.bitwise_xor(lax.axis_index("expert") // 2, mask)


def core_of():
    return lax.axis_index("expert") % 2


def norm_kernel(tokens_ref, *refs):
    mine_ref, other_ref, scratch = refs[-3:]
    scratch[...] = layer_norm(tokens_ref[...].astype(F32)).astype(BF16)
    core = core_of()
    block = mine_ref.shape[1] // CHIPS
    for at in range(CHIPS):
        start = pl.multiple_of(chip_of(at) * block, block)
        columns = scratch[:, pl.ds(start, block)]
        swapped = pltpu.roll(columns.astype(F32), block // 2, 1).astype(BF16)
        place = slice(at * block, (at + 1) * block)
        mine_ref[:, place] = jnp.where(core == 0, columns, swapped)
        other_ref[:, place] = jnp.where(core == 0, swapped, columns)


def norm(tokens, image, length, before, others=(), cost=0):
    rows, width = tokens.shape
    piece = pl.BlockSpec((length, width), lambda step: (image, 0))
    return pl.pallas_call(
        norm_kernel,
        out_shape=[jax.ShapeDtypeStruct((rows, width), BF16)] * 2,
        grid=(1,),
        in_specs=[piece] + [pl.BlockSpec(memory_space=pl.ANY)] * len((*others, *before)),
        out_specs=[piece] * 2,
        scratch_shapes=[pltpu.VMEM((length, width), BF16)],
        input_output_aliases={1: 0, 2: 1} if others else {},
        compiler_params=pltpu.CompilerParams(vmem_limit_bytes=16 << 20),
        cost_estimate=pl.CostEstimate(
            flops=cost or 8 * length * width,
            bytes_accessed=6 * length * width,
            transcendentals=length,
        ),
        name="norm",
    )(tokens, *others, *before)


def copy_kernel(count, *refs):
    for source, target in zip(refs[:count], refs[-count:]):
        target[...] = source[...]


def copies(values, before):
    vmem = pl.BlockSpec(memory_space=pltpu.VMEM)
    return pl.pallas_call(
        functools.partial(copy_kernel, len(values)),
        out_shape=[jax.ShapeDtypeStruct(value.shape, value.dtype) for value in values],
        in_specs=[vmem] * len(values) + [pl.BlockSpec(memory_space=pl.ANY)] * len(before),
        out_specs=[vmem] * len(values),
        compiler_params=pltpu.CompilerParams(vmem_limit_bytes=4 << 20),
        cost_estimate=pl.CostEstimate(flops=0, bytes_accessed=0, transcendentals=0),
        name="copies",
    )(*values, *before)


def split_kernel(mine_ref, other_ref, *refs):
    span = mine_ref.shape[1] // 12
    rows = mine_ref.shape[0]
    for side, source in enumerate((mine_ref, other_ref)):
        for chunk in range(2):
            for which in range(3):
                start = (which * 4 + core_of() * 2 + chunk) * span
                refs[chunk - 2][
                    side * rows : (side + 1) * rows, which * span : (which + 1) * span
                ] = source[:, pl.ds(pl.multiple_of(start, span), span)]


def split_out_kernel(mine_ref, other_ref, *refs):
    span = mine_ref.shape[1] // 2
    rows = mine_ref.shape[0]
    for side, source in enumerate((mine_ref, other_ref)):
        start = pl.multiple_of(core_of() * span, span)
        refs[-1][side * rows : (side + 1) * rows] = source[:, pl.ds(start, span)]


def split(kernel, mine, other, count, columns, before=()):
    rows = mine.shape[0]
    vmem = pl.BlockSpec(memory_space=pltpu.VMEM)
    return pl.pallas_call(
        kernel,
        out_shape=[jax.ShapeDtypeStruct((2 * rows, columns), BF16)] * count,
        in_specs=[vmem] * 2 + [pl.BlockSpec(memory_space=pl.ANY)] * len(before),
        out_specs=[vmem] * count,
        compiler_params=pltpu.CompilerParams(vmem_limit_bytes=8 << 20),
        cost_estimate=pl.CostEstimate(
            flops=0, bytes_accessed=8 * rows * columns, transcendentals=0
        ),
        name="split",
    )(mine, other, *before)


def attend(query, keys, values, head, out_ref, rows, columns):
    lane = lax.broadcasted_iota(jnp.int32, query.shape, 1)
    first = lane < head
    result = []
    for mask in (first, ~first):
        scores = lax.dot_general(
            jnp.where(mask, query, jnp.zeros_like(query)),
            keys,
            (((1,), (1,)), ((), ())),
            preferred_element_type=F32,
        )
        top = jnp.max(scores, axis=-1, keepdims=True)
        weights = jnp.exp(scores - top).astype(BF16)
        mixed = jnp.dot(
            weights, jnp.where(mask, values, jnp.ones_like(values)), preferred_element_type=F32
        )
        result.append(mixed / pltpu.roll(mixed, head, 1))
    out_ref[rows, columns] = jnp.where(first, result[0], result[1]).astype(BF16)


def attention_kernel(length, head, normed, weight, *refs):
    out_ref = refs[-1]
    span = out_ref.shape[1]
    pair = 2 * head

    def project(at):
        return jnp.dot(
            normed[...], weight[:, at * span : (at + 1) * span], preferred_element_type=F32
        )

    query = (project(0) * head**-0.5).astype(BF16)
    keys = project(1).astype(BF16)
    values = project(2).astype(BF16)
    for start in range(0, normed.shape[0], length):
        rows = slice(start, start + length)
        for left in range(0, span, pair):
            columns = slice(left, left + pair)
            attend(
                query[rows, columns],
                keys[rows, columns],
                values[rows, columns],
                head,
                out_ref,
                rows,
                columns,
            )


def attention(normed, weight, length, head, before=()):
    rows, width = normed.shape
    span = weight.shape[1] // 3
    vmem = pl.BlockSpec(memory_space=pltpu.VMEM)
    return pl.pallas_call(
        functools.partial(attention_kernel, length, head),
        out_shape=jax.ShapeDtypeStruct((rows, span), BF16),
        in_specs=[vmem] * 2 + [pl.BlockSpec(memory_space=pl.ANY)] * len(before),
        out_specs=vmem,
        compiler_params=pltpu.CompilerParams(vmem_limit_bytes=20 << 20),
        cost_estimate=pl.CostEstimate(
            flops=2 * rows * span * (3 * width + 2 * length),
            bytes_accessed=6 * width * span + 4 * rows * width,
            transcendentals=rows * (span // head) * length,
        ),
        name="attention",
    )(normed, weight, *before)


def router_kernel(count, images, length, *refs):
    tokens_ref, keys_ref = refs[:2]
    parts = refs[2:6]
    sources = refs[6:10]
    resid_ref, combine_ref, inputs_ref = refs[10:13]
    weight, sem = refs[13:]
    core = core_of()
    span = sources[0].shape[1]
    half = weight.shape[0] // (2 * count)
    copies = []
    for which, source in enumerate(sources):
        side = which // 2
        left = pl.multiple_of(jnp.bitwise_xor(core, side) * span, span)
        for at, block in enumerate((EARLY, LATE)[which % 2]):
            for part in range(2):
                start = (2 * chip_of(block) + jnp.bitwise_xor(core, part ^ side)) * half
                copy = pltpu.make_async_copy(
                    source.at[pl.ds((2 * at + part) * half, half)],
                    weight.at[pl.ds(pl.multiple_of(start, half), half), pl.ds(left, span)],
                    sem.at[len(copies)],
                )
                copy.start()
                copies.append(copy)
    for copy in copies:
        copy.wait()
    inner = parts[0].shape[1]
    for image in range(images):
        at = slice(image * length, (image + 1) * length)
        resid = tokens_ref[at].astype(F32)
        for which, part in enumerate(parts):
            side, chunk = which // 2, which % 2
            start = (2 * jnp.bitwise_xor(core, side) + chunk) * inner
            resid += jnp.dot(
                part[at],
                weight[pl.ds(pl.multiple_of(start, inner), inner)],
                preferred_element_type=F32,
            )
        resid_ref[at] = resid
        normed = layer_norm(resid).astype(BF16)
        logits = lax.dot_general(
            keys_ref[...], normed, (((1,), (1,)), ((), ())), preferred_element_type=F32
        )
        dispatch = jax.nn.softmax(logits, axis=1).astype(BF16)
        combine_ref[image] = jax.nn.softmax(logits, axis=0).astype(BF16)
        inputs_ref[image] = jnp.dot(dispatch, normed, preferred_element_type=F32).astype(BF16)


def router(tokens, slot_keys, parts, blocks, images, length):
    rows, width = tokens.shape
    slots = slot_keys.shape[1]
    count = CHIPS
    vmem = pl.BlockSpec(memory_space=pltpu.VMEM)
    hbm = pl.BlockSpec(memory_space=pl.ANY)
    return pl.pallas_call(
        functools.partial(router_kernel, count, images, length),
        out_shape=[
            jax.ShapeDtypeStruct((rows, width), F32),
            jax.ShapeDtypeStruct((images, slots, length), BF16),
            jax.ShapeDtypeStruct((images, slots, width), BF16),
        ],
        in_specs=[vmem] * 6 + [hbm] * 4,
        out_specs=[vmem] * 3,
        scratch_shapes=[
            pltpu.VMEM((width, width), BF16),
            pltpu.SemaphoreType.DMA((4 * count,)),
        ],
        compiler_params=pltpu.CompilerParams(vmem_limit_bytes=24 << 20),
        cost_estimate=pl.CostEstimate(
            flops=2 * rows * width * (width + 2 * slots),
            bytes_accessed=2 * width * width + 8 * rows * width,
            transcendentals=2 * rows * slots,
        ),
        name="router",
    )(tokens, slot_keys.T, *parts, *blocks)


def expert_kernel(inputs_ref, first_ref, second_ref, out_ref, total):
    step = pl.program_id(1)
    hidden = jnp.dot(inputs_ref[0], first_ref[0], preferred_element_type=F32)
    hidden = (0.5 * hidden * (1.0 + lax.erf(hidden * 0.5**0.5))).astype(BF16)
    answer = jnp.dot(hidden, second_ref[0], preferred_element_type=F32)

    @pl.when(step == 0)
    def _():
        total[...] = answer

    @pl.when(step > 0)
    def _():
        total[...] += answer

    @pl.when(step == pl.num_programs(1) - 1)
    def _():
        out_ref[0] = total[...].astype(BF16)


def experts_here(inputs, first, second):
    count, rows, width = inputs.shape
    hidden = first.shape[2]
    piece = hidden // EXPERT_STEPS
    return pl.pallas_call(
        expert_kernel,
        out_shape=jax.ShapeDtypeStruct(inputs.shape, BF16),
        grid=(count, EXPERT_STEPS),
        in_specs=[
            pl.BlockSpec((1, rows, width), lambda e, h: (e, 0, 0)),
            pl.BlockSpec((1, width, piece), lambda e, h: (e, 0, h)),
            pl.BlockSpec((1, piece, width), lambda e, h: (e, h, 0)),
        ],
        out_specs=pl.BlockSpec((1, rows, width), lambda e, h: (e, 0, 0)),
        scratch_shapes=[pltpu.VMEM((rows, width), F32)],
        compiler_params=pltpu.CompilerParams(vmem_limit_bytes=24 << 20),
        cost_estimate=pl.CostEstimate(
            flops=4 * count * rows * width * hidden,
            bytes_accessed=4 * count * width * hidden,
            transcendentals=count * rows * hidden,
        ),
        name="experts",
    )(inputs, first, second)


def front_on_grid(groups, experts, tokens, w_qkv, w_attn_out, slot_keys):
    images, length, width = tokens.shape
    head = width // HEADS
    flat = tokens.reshape(images * length, width)
    def send(value, move):
        pairs = []
        for at in range(groups):
            mask, flip = move(at)
            for index in range(experts):
                target = (at ^ flip) * experts + (index ^ mask)
                pairs.append((at * experts + index, target))
        return lax.ppermute(value, AXES, pairs)

    def in_chip(value):
        return send(value, lambda at: (1, 0))

    def over_y(value):
        return send(value, lambda at: (2, 0))

    def near_z(value):
        return send(value, lambda at: (4, 0))

    def far_z(value):
        return send(value, lambda at: (12, 0) if at else (8, 0))

    def over_x(value):
        return send(value, lambda at: (0, 1))

    span = width // 4
    a, b = split(split_kernel, w_qkv, in_chip(w_qkv), 2, 3 * span)

    def whole(*blocks):
        return jnp.concatenate(blocks, axis=0)

    def step(*values, done=()):
        nonlocal token
        *result, token = copies([*values, token], done)
        return result

    a_far = far_z(a)
    a_near = near_z(a)
    a_y = over_y(a)
    normed, normed_sent = norm(flat, 0, length, (a,), cost=LONG)
    token = normed[:8, :128]
    (b_1,) = step(b)
    b_y = over_y(b_1)
    a_far_1, b_2 = step(a_far, b, done=(a_y, a_near))
    b_far = far_z(b_2)
    a_x = over_x(a_far_1)
    a_y_far = over_y(a_far_1)
    (a_near_1,) = step(a_near, done=(b_y,))
    a_y_near = over_y(a_near_1)
    for image in range(1, images):
        normed, normed_sent = norm(flat, image, length, (token,), (normed, normed_sent), LONG)
    (a_y_far_1,) = step(a_y_far)
    a_x_far = over_x(a_y_far_1)
    (w_out,) = step(w_attn_out)
    (c,) = split(split_out_kernel, w_out, in_chip(w_out), 1, 2 * span)
    b_3, c_1 = step(b, c, done=(a_x,))
    b_near = near_z(b_3)
    c_y = over_y(c_1)
    normed_other = in_chip(normed_sent)
    b_far_1, c_2 = step(b_far, c, done=(a_y_near, a_x_far))
    b_x = over_x(b_far_1)
    b_y_far = over_y(b_far_1)
    c_far = far_z(c_2)
    a_all = whole(a, a_y, a_near, a_y_near, a_far, a_x, a_y_far, a_x_far)
    other_a = attention(normed_other, a_all, length, head, (token,))
    (b_near_1,) = step(b_near, done=(other_a, c_y))
    b_y_near = over_y(b_near_1)
    (b_y_far_1,) = step(b_y_far)
    b_x_far = over_x(b_y_far_1)
    (c_3,) = step(c, done=(b_x,))
    c_near = near_z(c_3)
    (c_far_1,) = step(c_far)
    c_y_far = over_y(c_far_1)
    c_x = over_x(c_far_1)
    mine_a = attention(normed, a_all, length, head, (token,))
    (c_near_1,) = step(c_near, done=(b_y_near, mine_a))
    c_y_near = over_y(c_near_1)
    (c_y_far_1,) = step(c_y_far)
    c_x_far = over_x(c_y_far_1)
    (other_a_1,) = step(other_a, done=(b_x_far,))
    parts_a = in_chip(other_a_1)
    b_all = whole(b, b_y, b_near, b_y_near, b_far, b_x, b_y_far, b_x_far)
    other_b = attention(normed_other, b_all, length, head, (token,))
    early = whole(c, c_y, c_near, c_far, c_y_far)
    late = whole(c_y_near, c_x, c_x_far, jnp.concatenate([other_b[:16], other_b[16:32]], axis=1))
    parts_b = in_chip(other_b)
    mine_b = attention(normed, b_all, length, head, (other_b,))
    parts = [mine_a, mine_b, parts_a, parts_b]
    outs = [early, late, in_chip(early), in_chip(late)]
    return router(flat, slot_keys, parts, outs, images, length)


def front(tokens, w_qkv, w_attn_out, slot_keys):
    images, length, width = tokens.shape
    head = width // HEADS
    rows = images * length
    normed = layer_norm(tokens.astype(F32)).astype(BF16).reshape(rows, width)
    full_qkv = lax.all_gather(w_qkv, "expert", axis=0, tiled=True)
    qkv = jnp.dot(normed, full_qkv, preferred_element_type=F32).astype(BF16)
    query, keys, values = [
        part[:, :, 0] for part in jnp.split(qkv.reshape(images, length, 3, HEADS, head), 3, axis=2)
    ]
    scores = jnp.einsum("bqhd,bkhd->bhqk", query, keys, preferred_element_type=F32) * head**-0.5
    weights = jax.nn.softmax(scores, axis=-1).astype(BF16)
    attended = jnp.einsum("bhqk,bkhd->bqhd", weights, values, preferred_element_type=F32)
    full_out = lax.all_gather(w_attn_out, "expert", axis=0, tiled=True)
    projected = jnp.dot(
        attended.astype(BF16).reshape(rows, width), full_out, preferred_element_type=F32
    )
    resid = tokens.astype(F32).reshape(rows, width) + projected
    normed_two = layer_norm(resid).astype(BF16).reshape(images, length, width)
    logits = jnp.einsum("bsd,dn->bns", normed_two, slot_keys, preferred_element_type=F32)
    dispatch = jax.nn.softmax(logits, axis=2).astype(BF16)
    combine = jax.nn.softmax(logits, axis=1).astype(BF16)
    slot_inputs = jnp.einsum("bns,bsd->bnd", dispatch, normed_two, preferred_element_type=F32)
    return resid, combine, slot_inputs.astype(BF16)


def on_device(mesh_shape, tokens, w_qkv, w_attn_out, slot_keys, w_expert_in, w_expert_out):
    images, length, width = tokens.shape
    if is_grid(*mesh_shape):
        resid, combine, slot_inputs = front_on_grid(
            *mesh_shape, tokens, w_qkv, w_attn_out, slot_keys
        )
    else:
        resid, combine, slot_inputs = front(tokens, w_qkv, w_attn_out, slot_keys)
    slots = slot_keys.shape[1]
    sources = mesh_shape[1]
    expert_here = w_expert_in.shape[0]
    pairs = slots // (sources * expert_here)
    block = lax.all_to_all(slot_inputs, "expert", split_axis=1, concat_axis=1, tiled=True)
    arranged = block.reshape(images, sources, expert_here, pairs, width)
    arranged = arranged.transpose(2, 0, 1, 3, 4).reshape(expert_here, -1, width)
    answer = experts_here(arranged, w_expert_in, w_expert_out)
    answer = answer.reshape(expert_here, images, sources, pairs, width)
    answered = answer.transpose(1, 2, 0, 3, 4).reshape(images, slots, width)
    slot_outputs = lax.all_to_all(answered, "expert", split_axis=1, concat_axis=1, tiled=True)
    mixed = jnp.einsum("bns,bnd->bsd", combine, slot_outputs, preferred_element_type=F32)
    return (resid.reshape(images, length, width) + mixed).astype(BF16)


def solution(mesh):
    placed = (
        P(AXES, None, None),
        P("expert", None),
        P("expert", None),
        P(),
        P("expert", None, None),
        P("expert", None, None),
    )
    return jax.shard_map(
        functools.partial(on_device, (mesh.shape["group"], mesh.shape["expert"])),
        mesh=mesh,
        in_specs=placed,
        out_specs=P(AXES, None, None),
        check_vma=False,
    )
```

```python
import functools

import jax
import jax.numpy as jnp
from jax import lax
from jax.experimental import pallas as pl
from jax.experimental.pallas import tpu as pltpu
from jax.sharding import PartitionSpec as P

HEADS = 16
EXPERT_STEPS = 2
CHIPS = 8
LONG = 1 << 34
EARLY = (0, 1, 2, 4, 6)
LATE = (3, 5, 7)
AXES = ("group", "expert")
F32 = jnp.float32
BF16 = jnp.bfloat16


def layer_norm(values):
    center = values - jnp.mean(values, axis=-1, keepdims=True)
    spread = jnp.mean(center * center, axis=-1, keepdims=True)
    return center * lax.rsqrt(spread + 1e-06)


def is_grid(groups, experts):
    return groups == 2 and experts == 16


def chip_of(block):
    far = lax.axis_index("group") * 2
    mask = (block, block, block, block, 4 + far, 6 - far, 5 + far, 7 - far)[block]
    return jnp.bitwise_xor(lax.axis_index("expert") // 2, mask)


def core_of():
    return lax.axis_index("expert") % 2


def norm_kernel(tokens_ref, *refs):
    mine_ref, other_ref, scratch = refs[-3:]
    scratch[...] = layer_norm(tokens_ref[...].astype(F32)).astype(BF16)
    core = core_of()
    block = mine_ref.shape[1] // CHIPS
    for at in range(CHIPS):
        start = pl.multiple_of(chip_of(at) * block, block)
        columns = scratch[:, pl.ds(start, block)]
        swapped = pltpu.roll(columns.astype(F32), block // 2, 1).astype(BF16)
        place = slice(at * block, (at + 1) * block)
        mine_ref[:, place] = jnp.where(core == 0, columns, swapped)
        other_ref[:, place] = jnp.where(core == 0, swapped, columns)


def norm(tokens, image, length, before, others=(), cost=0):
    rows, width = tokens.shape
    piece = pl.BlockSpec((length, width), lambda step: (image, 0))
    return pl.pallas_call(
        norm_kernel,
        out_shape=[jax.ShapeDtypeStruct((rows, width), BF16)] * 2,
        grid=(1,),
        in_specs=[piece] + [pl.BlockSpec(memory_space=pl.ANY)] * len((*others, *before)),
        out_specs=[piece] * 2,
        scratch_shapes=[pltpu.VMEM((length, width), BF16)],
        input_output_aliases={1: 0, 2: 1} if others else {},
        compiler_params=pltpu.CompilerParams(vmem_limit_bytes=16 << 20),
        cost_estimate=pl.CostEstimate(
            flops=cost or 8 * length * width,
            bytes_accessed=6 * length * width,
            transcendentals=length,
        ),
        name="norm",
    )(tokens, *others, *before)


def copy_kernel(count, *refs):
    for source, target in zip(refs[:count], refs[-count:]):
        target[...] = source[...]


def copies(values, before):
    vmem = pl.BlockSpec(memory_space=pltpu.VMEM)
    return pl.pallas_call(
        functools.partial(copy_kernel, len(values)),
        out_shape=[jax.ShapeDtypeStruct(value.shape, value.dtype) for value in values],
        in_specs=[vmem] * len(values) + [pl.BlockSpec(memory_space=pl.ANY)] * len(before),
        out_specs=[vmem] * len(values),
        compiler_params=pltpu.CompilerParams(vmem_limit_bytes=4 << 20),
        cost_estimate=pl.CostEstimate(flops=0, bytes_accessed=0, transcendentals=0),
        name="copies",
    )(*values, *before)


def split_kernel(mine_ref, other_ref, *refs):
    span = mine_ref.shape[1] // 12
    rows = mine_ref.shape[0]
    for side, source in enumerate((mine_ref, other_ref)):
        for chunk in range(2):
            for which in range(3):
                start = (which * 4 + core_of() * 2 + chunk) * span
                refs[chunk - 2][
                    side * rows : (side + 1) * rows, which * span : (which + 1) * span
                ] = source[:, pl.ds(pl.multiple_of(start, span), span)]


def split_out_kernel(mine_ref, other_ref, *refs):
    span = mine_ref.shape[1] // 2
    rows = mine_ref.shape[0]
    for side, source in enumerate((mine_ref, other_ref)):
        start = pl.multiple_of(core_of() * span, span)
        refs[-1][side * rows : (side + 1) * rows] = source[:, pl.ds(start, span)]


def split(kernel, mine, other, count, columns, before=()):
    rows = mine.shape[0]
    vmem = pl.BlockSpec(memory_space=pltpu.VMEM)
    return pl.pallas_call(
        kernel,
        out_shape=[jax.ShapeDtypeStruct((2 * rows, columns), BF16)] * count,
        in_specs=[vmem] * 2 + [pl.BlockSpec(memory_space=pl.ANY)] * len(before),
        out_specs=[vmem] * count,
        compiler_params=pltpu.CompilerParams(vmem_limit_bytes=8 << 20),
        cost_estimate=pl.CostEstimate(
            flops=0, bytes_accessed=8 * rows * columns, transcendentals=0
        ),
        name="split",
    )(mine, other, *before)


def attend(query, keys, values, head, out_ref, rows, columns):
    lane = lax.broadcasted_iota(jnp.int32, query.shape, 1)
    first = lane < head
    result = []
    for mask in (first, ~first):
        scores = lax.dot_general(
            jnp.where(mask, query, jnp.zeros_like(query)),
            keys,
            (((1,), (1,)), ((), ())),
            preferred_element_type=F32,
        )
        top = jnp.max(scores, axis=-1, keepdims=True)
        weights = jnp.exp(scores - top).astype(BF16)
        mixed = jnp.dot(
            weights, jnp.where(mask, values, jnp.ones_like(values)), preferred_element_type=F32
        )
        result.append(mixed / pltpu.roll(mixed, head, 1))
    out_ref[rows, columns] = jnp.where(first, result[0], result[1]).astype(BF16)


def attention_kernel(length, head, normed, weight, *refs):
    out_ref = refs[-1]
    span = out_ref.shape[1]
    pair = 2 * head

    def project(at):
        return jnp.dot(
            normed[...], weight[:, at * span : (at + 1) * span], preferred_element_type=F32
        )

    query = (project(0) * head**-0.5).astype(BF16)
    keys = project(1).astype(BF16)
    values = project(2).astype(BF16)
    for start in range(0, normed.shape[0], length):
        rows = slice(start, start + length)
        for left in range(0, span, pair):
            columns = slice(left, left + pair)
            attend(
                query[rows, columns],
                keys[rows, columns],
                values[rows, columns],
                head,
                out_ref,
                rows,
                columns,
            )


def attention(normed, weight, length, head, before=()):
    rows, width = normed.shape
    span = weight.shape[1] // 3
    vmem = pl.BlockSpec(memory_space=pltpu.VMEM)
    return pl.pallas_call(
        functools.partial(attention_kernel, length, head),
        out_shape=jax.ShapeDtypeStruct((rows, span), BF16),
        in_specs=[vmem] * 2 + [pl.BlockSpec(memory_space=pl.ANY)] * len(before),
        out_specs=vmem,
        compiler_params=pltpu.CompilerParams(vmem_limit_bytes=20 << 20),
        cost_estimate=pl.CostEstimate(
            flops=2 * rows * span * (3 * width + 2 * length),
            bytes_accessed=6 * width * span + 4 * rows * width,
            transcendentals=rows * (span // head) * length,
        ),
        name="attention",
    )(normed, weight, *before)


def router_kernel(count, images, length, *refs):
    tokens_ref, keys_ref = refs[:2]
    parts = refs[2:6]
    sources = refs[6:10]
    resid_ref, combine_ref, inputs_ref = refs[10:13]
    weight, sem = refs[13:]
    core = core_of()
    span = sources[0].shape[1]
    half = weight.shape[0] // (2 * count)
    copies = []
    for which, source in enumerate(sources):
        side = which // 2
        left = pl.multiple_of(jnp.bitwise_xor(core, side) * span, span)
        for at, block in enumerate((EARLY, LATE)[which % 2]):
            for part in range(2):
                start = (2 * chip_of(block) + jnp.bitwise_xor(core, part ^ side)) * half
                copy = pltpu.make_async_copy(
                    source.at[pl.ds((2 * at + part) * half, half)],
                    weight.at[pl.ds(pl.multiple_of(start, half), half), pl.ds(left, span)],
                    sem.at[len(copies)],
                )
                copy.start()
                copies.append(copy)
    for copy in copies:
        copy.wait()
    inner = parts[0].shape[1]
    for image in range(images):
        at = slice(image * length, (image + 1) * length)
        resid = tokens_ref[at].astype(F32)
        for which, part in enumerate(parts):
            side, chunk = which // 2, which % 2
            start = (2 * jnp.bitwise_xor(core, side) + chunk) * inner
            resid += jnp.dot(
                part[at],
                weight[pl.ds(pl.multiple_of(start, inner), inner)],
                preferred_element_type=F32,
            )
        resid_ref[at] = resid
        normed = layer_norm(resid).astype(BF16)
        logits = lax.dot_general(
            keys_ref[...], normed, (((1,), (1,)), ((), ())), preferred_element_type=F32
        )
        dispatch = jax.nn.softmax(logits, axis=1).astype(BF16)
        combine_ref[image] = jax.nn.softmax(logits, axis=0).astype(BF16)
        inputs_ref[image] = jnp.dot(dispatch, normed, preferred_element_type=F32).astype(BF16)


def router(tokens, slot_keys, parts, blocks, images, length):
    rows, width = tokens.shape
    slots = slot_keys.shape[1]
    count = CHIPS
    vmem = pl.BlockSpec(memory_space=pltpu.VMEM)
    hbm = pl.BlockSpec(memory_space=pl.ANY)
    return pl.pallas_call(
        functools.partial(router_kernel, count, images, length),
        out_shape=[
            jax.ShapeDtypeStruct((rows, width), F32),
            jax.ShapeDtypeStruct((images, slots, length), BF16),
            jax.ShapeDtypeStruct((images, slots, width), BF16),
        ],
        in_specs=[vmem] * 6 + [hbm] * 4,
        out_specs=[vmem] * 3,
        scratch_shapes=[
            pltpu.VMEM((width, width), BF16),
            pltpu.SemaphoreType.DMA((4 * count,)),
        ],
        compiler_params=pltpu.CompilerParams(vmem_limit_bytes=24 << 20),
        cost_estimate=pl.CostEstimate(
            flops=2 * rows * width * (width + 2 * slots),
            bytes_accessed=2 * width * width + 8 * rows * width,
            transcendentals=2 * rows * slots,
        ),
        name="router",
    )(tokens, slot_keys.T, *parts, *blocks)


def expert_kernel(inputs_ref, first_ref, second_ref, out_ref, total):
    step = pl.program_id(1)
    hidden = jnp.dot(inputs_ref[0], first_ref[0], preferred_element_type=F32)
    hidden = (0.5 * hidden * (1.0 + lax.erf(hidden * 0.5**0.5))).astype(BF16)
    answer = jnp.dot(hidden, second_ref[0], preferred_element_type=F32)

    @pl.when(step == 0)
    def _():
        total[...] = answer

    @pl.when(step > 0)
    def _():
        total[...] += answer

    @pl.when(step == pl.num_programs(1) - 1)
    def _():
        out_ref[0] = total[...].astype(BF16)


def experts_here(inputs, first, second):
    count, rows, width = inputs.shape
    hidden = first.shape[2]
    piece = hidden // EXPERT_STEPS
    return pl.pallas_call(
        expert_kernel,
        out_shape=jax.ShapeDtypeStruct(inputs.shape, BF16),
        grid=(count, EXPERT_STEPS),
        in_specs=[
            pl.BlockSpec((1, rows, width), lambda e, h: (e, 0, 0)),
            pl.BlockSpec((1, width, piece), lambda e, h: (e, 0, h)),
            pl.BlockSpec((1, piece, width), lambda e, h: (e, h, 0)),
        ],
        out_specs=pl.BlockSpec((1, rows, width), lambda e, h: (e, 0, 0)),
        scratch_shapes=[pltpu.VMEM((rows, width), F32)],
        compiler_params=pltpu.CompilerParams(vmem_limit_bytes=24 << 20),
        cost_estimate=pl.CostEstimate(
            flops=4 * count * rows * width * hidden,
            bytes_accessed=4 * count * width * hidden,
            transcendentals=count * rows * hidden,
        ),
        name="experts",
    )(inputs, first, second)


def front_on_grid(groups, experts, tokens, w_qkv, w_attn_out, slot_keys):
    images, length, width = tokens.shape
    head = width // HEADS
    flat = tokens.reshape(images * length, width)
    def send(value, move):
        pairs = []
        for at in range(groups):
            mask, flip = move(at)
            for index in range(experts):
                target = (at ^ flip) * experts + (index ^ mask)
                pairs.append((at * experts + index, target))
        return lax.ppermute(value, AXES, pairs)

    def in_chip(value):
        return send(value, lambda at: (1, 0))

    def over_y(value):
        return send(value, lambda at: (2, 0))

    def near_z(value):
        return send(value, lambda at: (4, 0))

    def far_z(value):
        return send(value, lambda at: (12, 0) if at else (8, 0))

    def over_x(value):
        return send(value, lambda at: (0, 1))

    span = width // 4
    a, b = split(split_kernel, w_qkv, in_chip(w_qkv), 2, 3 * span)

    def whole(*blocks):
        return jnp.concatenate(blocks, axis=0)

    def step(*values, done=()):
        nonlocal token
        *result, token = copies([*values, token], done)
        return result

    a_far = far_z(a)
    a_near = near_z(a)
    a_y = over_y(a)
    normed, normed_sent = norm(flat, 0, length, (a,), cost=LONG)
    token = normed[:8, :128]
    (b_1,) = step(b)
    b_y = over_y(b_1)
    a_far_1, b_2 = step(a_far, b, done=(a_y, a_near))
    b_far = far_z(b_2)
    a_x = over_x(a_far_1)
    a_y_far = over_y(a_far_1)
    (a_near_1,) = step(a_near, done=(b_y,))
    a_y_near = over_y(a_near_1)
    for image in range(1, images):
        normed, normed_sent = norm(flat, image, length, (token,), (normed, normed_sent), LONG)
    (a_y_far_1,) = step(a_y_far)
    a_x_far = over_x(a_y_far_1)
    (w_out,) = step(w_attn_out)
    (c,) = split(split_out_kernel, w_out, in_chip(w_out), 1, 2 * span)
    (b_3,) = step(b, done=(a_x,))
    b_near = near_z(b_3)
    normed_other = in_chip(normed_sent)
    b_far_1, c_2 = step(b_far, c, done=(a_y_near, a_x_far))
    b_x = over_x(b_far_1)
    b_y_far = over_y(b_far_1)
    c_far = far_z(c_2)
    a_all = whole(a, a_y, a_near, a_y_near, a_far, a_x, a_y_far, a_x_far)
    other_a = attention(normed_other, a_all, length, head, (token,))
    (b_near_1,) = step(b_near, done=(other_a,))
    b_y_near = over_y(b_near_1)
    (b_y_far_1,) = step(b_y_far)
    b_x_far = over_x(b_y_far_1)
    (c_3,) = step(c, done=(b_x,))
    c_near = near_z(c_3)
    c_y = over_y(c_3)
    (c_far_1,) = step(c_far)
    c_y_far = over_y(c_far_1)
    c_x = over_x(c_far_1)
    mine_a = attention(normed, a_all, length, head, (token,))
    (c_near_1,) = step(c_near, done=(b_y_near, mine_a))
    c_y_near = over_y(c_near_1)
    (c_y_far_1,) = step(c_y_far)
    c_x_far = over_x(c_y_far_1)
    (other_a_1,) = step(other_a, done=(b_x_far,))
    parts_a = in_chip(other_a_1)
    b_all = whole(b, b_y, b_near, b_y_near, b_far, b_x, b_y_far, b_x_far)
    other_b = attention(normed_other, b_all, length, head, (token,))
    early = whole(c, c_y, c_near, c_far, c_y_far)
    late = whole(c_y_near, c_x, c_x_far, jnp.concatenate([other_b[:16], other_b[16:32]], axis=1))
    parts_b = in_chip(other_b)
    mine_b = attention(normed, b_all, length, head, (other_b,))
    parts = [mine_a, mine_b, parts_a, parts_b]
    outs = [early, late, in_chip(early), in_chip(late)]
    return router(flat, slot_keys, parts, outs, images, length)


def front(tokens, w_qkv, w_attn_out, slot_keys):
    images, length, width = tokens.shape
    head = width // HEADS
    rows = images * length
    normed = layer_norm(tokens.astype(F32)).astype(BF16).reshape(rows, width)
    full_qkv = lax.all_gather(w_qkv, "expert", axis=0, tiled=True)
    qkv = jnp.dot(normed, full_qkv, preferred_element_type=F32).astype(BF16)
    query, keys, values = [
        part[:, :, 0] for part in jnp.split(qkv.reshape(images, length, 3, HEADS, head), 3, axis=2)
    ]
    scores = jnp.einsum("bqhd,bkhd->bhqk", query, keys, preferred_element_type=F32) * head**-0.5
    weights = jax.nn.softmax(scores, axis=-1).astype(BF16)
    attended = jnp.einsum("bhqk,bkhd->bqhd", weights, values, preferred_element_type=F32)
    full_out = lax.all_gather(w_attn_out, "expert", axis=0, tiled=True)
    projected = jnp.dot(
        attended.astype(BF16).reshape(rows, width), full_out, preferred_element_type=F32
    )
    resid = tokens.astype(F32).reshape(rows, width) + projected
    normed_two = layer_norm(resid).astype(BF16).reshape(images, length, width)
    logits = jnp.einsum("bsd,dn->bns", normed_two, slot_keys, preferred_element_type=F32)
    dispatch = jax.nn.softmax(logits, axis=2).astype(BF16)
    combine = jax.nn.softmax(logits, axis=1).astype(BF16)
    slot_inputs = jnp.einsum("bns,bsd->bnd", dispatch, normed_two, preferred_element_type=F32)
    return resid, combine, slot_inputs.astype(BF16)


def on_device(mesh_shape, tokens, w_qkv, w_attn_out, slot_keys, w_expert_in, w_expert_out):
    images, length, width = tokens.shape
    if is_grid(*mesh_shape):
        resid, combine, slot_inputs = front_on_grid(
            *mesh_shape, tokens, w_qkv, w_attn_out, slot_keys
        )
    else:
        resid, combine, slot_inputs = front(tokens, w_qkv, w_attn_out, slot_keys)
    slots = slot_keys.shape[1]
    sources = mesh_shape[1]
    expert_here = w_expert_in.shape[0]
    pairs = slots // (sources * expert_here)
    block = lax.all_to_all(slot_inputs, "expert", split_axis=1, concat_axis=1, tiled=True)
    arranged = block.reshape(images, sources, expert_here, pairs, width)
    arranged = arranged.transpose(2, 0, 1, 3, 4).reshape(expert_here, -1, width)
    answer = experts_here(arranged, w_expert_in, w_expert_out)
    answer = answer.reshape(expert_here, images, sources, pairs, width)
    answered = answer.transpose(1, 2, 0, 3, 4).reshape(images, slots, width)
    slot_outputs = lax.all_to_all(answered, "expert", split_axis=1, concat_axis=1, tiled=True)
    mixed = jnp.einsum("bns,bnd->bsd", combine, slot_outputs, preferred_element_type=F32)
    return (resid.reshape(images, length, width) + mixed).astype(BF16)


def solution(mesh):
    placed = (
        P(AXES, None, None),
        P("expert", None),
        P("expert", None),
        P(),
        P("expert", None, None),
        P("expert", None, None),
    )
    return jax.shard_map(
        functools.partial(on_device, (mesh.shape["group"], mesh.shape["expert"])),
        mesh=mesh,
        in_specs=placed,
        out_specs=P(AXES, None, None),
        check_vma=False,
    )
```

```python
import functools

import jax
import jax.numpy as jnp
from jax import lax
from jax.experimental import pallas as pl
from jax.experimental.pallas import tpu as pltpu
from jax.sharding import PartitionSpec as P

HEADS = 16
EXPERT_STEPS = 1
CHIPS = 8
LONG = 1 << 34
EARLY = (0, 1, 2, 4, 6)
LATE = (3, 5, 7)
AXES = ("group", "expert")
F32 = jnp.float32
BF16 = jnp.bfloat16


def layer_norm(values):
    center = values - jnp.mean(values, axis=-1, keepdims=True)
    spread = jnp.mean(center * center, axis=-1, keepdims=True)
    return center * lax.rsqrt(spread + 1e-06)


def is_grid(groups, experts):
    return groups == 2 and experts == 16


def chip_of(block):
    far = lax.axis_index("group") * 2
    mask = (block, block, block, block, 4 + far, 6 - far, 5 + far, 7 - far)[block]
    return jnp.bitwise_xor(lax.axis_index("expert") // 2, mask)


def core_of():
    return lax.axis_index("expert") % 2


def norm_kernel(tokens_ref, *refs):
    mine_ref, other_ref, scratch = refs[-3:]
    scratch[...] = layer_norm(tokens_ref[...].astype(F32)).astype(BF16)
    core = core_of()
    block = mine_ref.shape[1] // CHIPS
    for at in range(CHIPS):
        start = pl.multiple_of(chip_of(at) * block, block)
        columns = scratch[:, pl.ds(start, block)]
        swapped = pltpu.roll(columns.astype(F32), block // 2, 1).astype(BF16)
        place = slice(at * block, (at + 1) * block)
        mine_ref[:, place] = jnp.where(core == 0, columns, swapped)
        other_ref[:, place] = jnp.where(core == 0, swapped, columns)


def norm(tokens, image, length, before, others=(), cost=0):
    rows, width = tokens.shape
    piece = pl.BlockSpec((length, width), lambda step: (image, 0))
    return pl.pallas_call(
        norm_kernel,
        out_shape=[jax.ShapeDtypeStruct((rows, width), BF16)] * 2,
        grid=(1,),
        in_specs=[piece] + [pl.BlockSpec(memory_space=pl.ANY)] * len((*others, *before)),
        out_specs=[piece] * 2,
        scratch_shapes=[pltpu.VMEM((length, width), BF16)],
        input_output_aliases={1: 0, 2: 1} if others else {},
        compiler_params=pltpu.CompilerParams(vmem_limit_bytes=16 << 20),
        cost_estimate=pl.CostEstimate(
            flops=cost or 8 * length * width,
            bytes_accessed=6 * length * width,
            transcendentals=length,
        ),
        name="norm",
    )(tokens, *others, *before)


def copy_kernel(count, *refs):
    for source, target in zip(refs[:count], refs[-count:]):
        target[...] = source[...]


def copies(values, before):
    vmem = pl.BlockSpec(memory_space=pltpu.VMEM)
    return pl.pallas_call(
        functools.partial(copy_kernel, len(values)),
        out_shape=[jax.ShapeDtypeStruct(value.shape, value.dtype) for value in values],
        in_specs=[vmem] * len(values) + [pl.BlockSpec(memory_space=pl.ANY)] * len(before),
        out_specs=[vmem] * len(values),
        compiler_params=pltpu.CompilerParams(vmem_limit_bytes=4 << 20),
        cost_estimate=pl.CostEstimate(flops=0, bytes_accessed=0, transcendentals=0),
        name="copies",
    )(*values, *before)


def split_kernel(mine_ref, other_ref, *refs):
    span = mine_ref.shape[1] // 12
    rows = mine_ref.shape[0]
    for side, source in enumerate((mine_ref, other_ref)):
        for chunk in range(2):
            for which in range(3):
                start = (which * 4 + core_of() * 2 + chunk) * span
                refs[chunk - 2][
                    side * rows : (side + 1) * rows, which * span : (which + 1) * span
                ] = source[:, pl.ds(pl.multiple_of(start, span), span)]


def split_out_kernel(mine_ref, other_ref, *refs):
    span = mine_ref.shape[1] // 2
    rows = mine_ref.shape[0]
    for side, source in enumerate((mine_ref, other_ref)):
        start = pl.multiple_of(core_of() * span, span)
        refs[-1][side * rows : (side + 1) * rows] = source[:, pl.ds(start, span)]


def split(kernel, mine, other, count, columns, before=()):
    rows = mine.shape[0]
    vmem = pl.BlockSpec(memory_space=pltpu.VMEM)
    return pl.pallas_call(
        kernel,
        out_shape=[jax.ShapeDtypeStruct((2 * rows, columns), BF16)] * count,
        in_specs=[vmem] * 2 + [pl.BlockSpec(memory_space=pl.ANY)] * len(before),
        out_specs=[vmem] * count,
        compiler_params=pltpu.CompilerParams(vmem_limit_bytes=8 << 20),
        cost_estimate=pl.CostEstimate(
            flops=0, bytes_accessed=8 * rows * columns, transcendentals=0
        ),
        name="split",
    )(mine, other, *before)


def attend(query, keys, values, head, out_ref, rows, columns):
    lane = lax.broadcasted_iota(jnp.int32, query.shape, 1)
    first = lane < head
    result = []
    for mask in (first, ~first):
        scores = lax.dot_general(
            jnp.where(mask, query, jnp.zeros_like(query)),
            keys,
            (((1,), (1,)), ((), ())),
            preferred_element_type=F32,
        )
        top = jnp.max(scores, axis=-1, keepdims=True)
        weights = jnp.exp(scores - top).astype(BF16)
        mixed = jnp.dot(
            weights, jnp.where(mask, values, jnp.ones_like(values)), preferred_element_type=F32
        )
        result.append(mixed / pltpu.roll(mixed, head, 1))
    out_ref[rows, columns] = jnp.where(first, result[0], result[1]).astype(BF16)


def attention_kernel(length, head, normed, weight, *refs):
    out_ref = refs[-1]
    span = out_ref.shape[1]
    pair = 2 * head

    def project(at):
        return jnp.dot(
            normed[...], weight[:, at * span : (at + 1) * span], preferred_element_type=F32
        )

    query = (project(0) * head**-0.5).astype(BF16)
    keys = project(1).astype(BF16)
    values = project(2).astype(BF16)
    for start in range(0, normed.shape[0], length):
        rows = slice(start, start + length)
        for left in range(0, span, pair):
            columns = slice(left, left + pair)
            attend(
                query[rows, columns],
                keys[rows, columns],
                values[rows, columns],
                head,
                out_ref,
                rows,
                columns,
            )


def attention(normed, weight, length, head, before=()):
    rows, width = normed.shape
    span = weight.shape[1] // 3
    vmem = pl.BlockSpec(memory_space=pltpu.VMEM)
    return pl.pallas_call(
        functools.partial(attention_kernel, length, head),
        out_shape=jax.ShapeDtypeStruct((rows, span), BF16),
        in_specs=[vmem] * 2 + [pl.BlockSpec(memory_space=pl.ANY)] * len(before),
        out_specs=vmem,
        compiler_params=pltpu.CompilerParams(vmem_limit_bytes=20 << 20),
        cost_estimate=pl.CostEstimate(
            flops=2 * rows * span * (3 * width + 2 * length),
            bytes_accessed=6 * width * span + 4 * rows * width,
            transcendentals=rows * (span // head) * length,
        ),
        name="attention",
    )(normed, weight, *before)


def router_kernel(count, images, length, *refs):
    tokens_ref, keys_ref = refs[:2]
    parts = refs[2:6]
    sources = refs[6:10]
    resid_ref, combine_ref, inputs_ref = refs[10:13]
    weight, sem = refs[13:]
    core = core_of()
    span = sources[0].shape[1]
    half = weight.shape[0] // (2 * count)
    copies = []
    for which, source in enumerate(sources):
        side = which // 2
        left = pl.multiple_of(jnp.bitwise_xor(core, side) * span, span)
        for at, block in enumerate((EARLY, LATE)[which % 2]):
            for part in range(2):
                start = (2 * chip_of(block) + jnp.bitwise_xor(core, part ^ side)) * half
                copy = pltpu.make_async_copy(
                    source.at[pl.ds((2 * at + part) * half, half)],
                    weight.at[pl.ds(pl.multiple_of(start, half), half), pl.ds(left, span)],
                    sem.at[len(copies)],
                )
                copy.start()
                copies.append(copy)
    for copy in copies:
        copy.wait()
    inner = parts[0].shape[1]
    for image in range(images):
        at = slice(image * length, (image + 1) * length)
        resid = tokens_ref[at].astype(F32)
        for which, part in enumerate(parts):
            side, chunk = which // 2, which % 2
            start = (2 * jnp.bitwise_xor(core, side) + chunk) * inner
            resid += jnp.dot(
                part[at],
                weight[pl.ds(pl.multiple_of(start, inner), inner)],
                preferred_element_type=F32,
            )
        resid_ref[at] = resid
        normed = layer_norm(resid).astype(BF16)
        logits = lax.dot_general(
            keys_ref[...], normed, (((1,), (1,)), ((), ())), preferred_element_type=F32
        )
        dispatch = jax.nn.softmax(logits, axis=1).astype(BF16)
        combine_ref[image] = jax.nn.softmax(logits, axis=0).astype(BF16)
        inputs_ref[image] = jnp.dot(dispatch, normed, preferred_element_type=F32).astype(BF16)


def router(tokens, slot_keys, parts, blocks, images, length):
    rows, width = tokens.shape
    slots = slot_keys.shape[1]
    count = CHIPS
    vmem = pl.BlockSpec(memory_space=pltpu.VMEM)
    hbm = pl.BlockSpec(memory_space=pl.ANY)
    return pl.pallas_call(
        functools.partial(router_kernel, count, images, length),
        out_shape=[
            jax.ShapeDtypeStruct((rows, width), F32),
            jax.ShapeDtypeStruct((images, slots, length), BF16),
            jax.ShapeDtypeStruct((images, slots, width), BF16),
        ],
        in_specs=[vmem] * 6 + [hbm] * 4,
        out_specs=[vmem] * 3,
        scratch_shapes=[
            pltpu.VMEM((width, width), BF16),
            pltpu.SemaphoreType.DMA((4 * count,)),
        ],
        compiler_params=pltpu.CompilerParams(vmem_limit_bytes=24 << 20),
        cost_estimate=pl.CostEstimate(
            flops=2 * rows * width * (width + 2 * slots),
            bytes_accessed=2 * width * width + 8 * rows * width,
            transcendentals=2 * rows * slots,
        ),
        name="router",
    )(tokens, slot_keys.T, *parts, *blocks)


def expert_kernel(inputs_ref, first_ref, second_ref, out_ref, total):
    step = pl.program_id(1)
    hidden = jnp.dot(inputs_ref[0], first_ref[0], preferred_element_type=F32)
    hidden = (0.5 * hidden * (1.0 + lax.erf(hidden * 0.5**0.5))).astype(BF16)
    answer = jnp.dot(hidden, second_ref[0], preferred_element_type=F32)

    @pl.when(step == 0)
    def _():
        total[...] = answer

    @pl.when(step > 0)
    def _():
        total[...] += answer

    @pl.when(step == pl.num_programs(1) - 1)
    def _():
        out_ref[0] = total[...].astype(BF16)


def experts_here(inputs, first, second):
    count, rows, width = inputs.shape
    hidden = first.shape[2]
    piece = hidden // EXPERT_STEPS
    return pl.pallas_call(
        expert_kernel,
        out_shape=jax.ShapeDtypeStruct(inputs.shape, BF16),
        grid=(count, EXPERT_STEPS),
        in_specs=[
            pl.BlockSpec((1, rows, width), lambda e, h: (e, 0, 0)),
            pl.BlockSpec((1, width, piece), lambda e, h: (e, 0, h)),
            pl.BlockSpec((1, piece, width), lambda e, h: (e, h, 0)),
        ],
        out_specs=pl.BlockSpec((1, rows, width), lambda e, h: (e, 0, 0)),
        scratch_shapes=[pltpu.VMEM((rows, width), F32)],
        compiler_params=pltpu.CompilerParams(vmem_limit_bytes=24 << 20),
        cost_estimate=pl.CostEstimate(
            flops=4 * count * rows * width * hidden,
            bytes_accessed=4 * count * width * hidden,
            transcendentals=count * rows * hidden,
        ),
        name="experts",
    )(inputs, first, second)


def front_on_grid(groups, experts, tokens, w_qkv, w_attn_out, slot_keys):
    images, length, width = tokens.shape
    head = width // HEADS
    flat = tokens.reshape(images * length, width)
    def send(value, move):
        pairs = []
        for at in range(groups):
            mask, flip = move(at)
            for index in range(experts):
                target = (at ^ flip) * experts + (index ^ mask)
                pairs.append((at * experts + index, target))
        return lax.ppermute(value, AXES, pairs)

    def in_chip(value):
        return send(value, lambda at: (1, 0))

    def over_y(value):
        return send(value, lambda at: (2, 0))

    def near_z(value):
        return send(value, lambda at: (4, 0))

    def far_z(value):
        return send(value, lambda at: (12, 0) if at else (8, 0))

    def over_x(value):
        return send(value, lambda at: (0, 1))

    span = width // 4
    a, b = split(split_kernel, w_qkv, in_chip(w_qkv), 2, 3 * span)

    def whole(*blocks):
        return jnp.concatenate(blocks, axis=0)

    def step(*values, done=()):
        nonlocal token
        *result, token = copies([*values, token], done)
        return result

    a_far = far_z(a)
    a_near = near_z(a)
    a_y = over_y(a)
    normed, normed_sent = norm(flat, 0, length, (a,), cost=LONG)
    token = normed[:8, :128]
    (b_1,) = step(b)
    b_y = over_y(b_1)
    a_far_1, b_2 = step(a_far, b, done=(a_y, a_near))
    b_far = far_z(b_2)
    a_x = over_x(a_far_1)
    a_y_far = over_y(a_far_1)
    (a_near_1,) = step(a_near, done=(b_y,))
    a_y_near = over_y(a_near_1)
    for image in range(1, images):
        normed, normed_sent = norm(flat, image, length, (token,), (normed, normed_sent), LONG)
    (a_y_far_1,) = step(a_y_far)
    a_x_far = over_x(a_y_far_1)
    (w_out,) = step(w_attn_out)
    (c,) = split(split_out_kernel, w_out, in_chip(w_out), 1, 2 * span)
    (b_3,) = step(b, done=(a_x,))
    b_near = near_z(b_3)
    normed_other = in_chip(normed_sent)
    b_far_1, c_2 = step(b_far, c, done=(a_y_near, a_x_far))
    b_x = over_x(b_far_1)
    b_y_far = over_y(b_far_1)
    c_far = far_z(c_2)
    a_all = whole(a, a_y, a_near, a_y_near, a_far, a_x, a_y_far, a_x_far)
    other_a = attention(normed_other, a_all, length, head, (token,))
    (b_near_1,) = step(b_near, done=(other_a,))
    b_y_near = over_y(b_near_1)
    (b_y_far_1,) = step(b_y_far)
    b_x_far = over_x(b_y_far_1)
    (c_3,) = step(c, done=(b_x,))
    c_near = near_z(c_3)
    c_y = over_y(c_3)
    (c_far_1,) = step(c_far)
    c_y_far = over_y(c_far_1)
    c_x = over_x(c_far_1)
    mine_a = attention(normed, a_all, length, head, (token,))
    (c_near_1,) = step(c_near, done=(b_y_near, mine_a))
    c_y_near = over_y(c_near_1)
    (c_y_far_1,) = step(c_y_far)
    c_x_far = over_x(c_y_far_1)
    (other_a_1,) = step(other_a, done=(b_x_far,))
    parts_a = in_chip(other_a_1)
    b_all = whole(b, b_y, b_near, b_y_near, b_far, b_x, b_y_far, b_x_far)
    other_b = attention(normed_other, b_all, length, head, (token,))
    early = whole(c, c_y, c_near, c_far, c_y_far)
    late = whole(c_y_near, c_x, c_x_far, jnp.concatenate([other_b[:16], other_b[16:32]], axis=1))
    parts_b = in_chip(other_b)
    mine_b = attention(normed, b_all, length, head, (other_b,))
    parts = [mine_a, mine_b, parts_a, parts_b]
    outs = [early, late, in_chip(early), in_chip(late)]
    return router(flat, slot_keys, parts, outs, images, length)


def front(tokens, w_qkv, w_attn_out, slot_keys):
    images, length, width = tokens.shape
    head = width // HEADS
    rows = images * length
    normed = layer_norm(tokens.astype(F32)).astype(BF16).reshape(rows, width)
    full_qkv = lax.all_gather(w_qkv, "expert", axis=0, tiled=True)
    qkv = jnp.dot(normed, full_qkv, preferred_element_type=F32).astype(BF16)
    query, keys, values = [
        part[:, :, 0] for part in jnp.split(qkv.reshape(images, length, 3, HEADS, head), 3, axis=2)
    ]
    scores = jnp.einsum("bqhd,bkhd->bhqk", query, keys, preferred_element_type=F32) * head**-0.5
    weights = jax.nn.softmax(scores, axis=-1).astype(BF16)
    attended = jnp.einsum("bhqk,bkhd->bqhd", weights, values, preferred_element_type=F32)
    full_out = lax.all_gather(w_attn_out, "expert", axis=0, tiled=True)
    projected = jnp.dot(
        attended.astype(BF16).reshape(rows, width), full_out, preferred_element_type=F32
    )
    resid = tokens.astype(F32).reshape(rows, width) + projected
    normed_two = layer_norm(resid).astype(BF16).reshape(images, length, width)
    logits = jnp.einsum("bsd,dn->bns", normed_two, slot_keys, preferred_element_type=F32)
    dispatch = jax.nn.softmax(logits, axis=2).astype(BF16)
    combine = jax.nn.softmax(logits, axis=1).astype(BF16)
    slot_inputs = jnp.einsum("bns,bsd->bnd", dispatch, normed_two, preferred_element_type=F32)
    return resid, combine, slot_inputs.astype(BF16)


def on_device(mesh_shape, tokens, w_qkv, w_attn_out, slot_keys, w_expert_in, w_expert_out):
    images, length, width = tokens.shape
    if is_grid(*mesh_shape):
        resid, combine, slot_inputs = front_on_grid(
            *mesh_shape, tokens, w_qkv, w_attn_out, slot_keys
        )
    else:
        resid, combine, slot_inputs = front(tokens, w_qkv, w_attn_out, slot_keys)
    slots = slot_keys.shape[1]
    sources = mesh_shape[1]
    expert_here = w_expert_in.shape[0]
    pairs = slots // (sources * expert_here)
    block = lax.all_to_all(slot_inputs, "expert", split_axis=1, concat_axis=1, tiled=True)
    arranged = block.reshape(images, sources, expert_here, pairs, width)
    arranged = arranged.transpose(2, 0, 1, 3, 4).reshape(expert_here, -1, width)
    answer = experts_here(arranged, w_expert_in, w_expert_out)
    answer = answer.reshape(expert_here, images, sources, pairs, width)
    answered = answer.transpose(1, 2, 0, 3, 4).reshape(images, slots, width)
    slot_outputs = lax.all_to_all(answered, "expert", split_axis=1, concat_axis=1, tiled=True)
    mixed = jnp.einsum("bns,bnd->bsd", combine, slot_outputs, preferred_element_type=F32)
    return (resid.reshape(images, length, width) + mixed).astype(BF16)


def solution(mesh):
    placed = (
        P(AXES, None, None),
        P("expert", None),
        P("expert", None),
        P(),
        P("expert", None, None),
        P("expert", None, None),
    )
    return jax.shard_map(
        functools.partial(on_device, (mesh.shape["group"], mesh.shape["expert"])),
        mesh=mesh,
        in_specs=placed,
        out_specs=P(AXES, None, None),
        check_vma=False,
    )
```

```python
import functools

import jax
import jax.numpy as jnp
from jax import lax
from jax.experimental import pallas as pl
from jax.experimental.pallas import tpu as pltpu
from jax.sharding import PartitionSpec as P

HEADS = 16
EXPERT_STEPS = 1
CHIPS = 8
LONG = 1 << 34
EARLY = (0, 1, 2, 4, 6)
LATE = (3, 5, 7)
AXES = ("group", "expert")
F32 = jnp.float32
BF16 = jnp.bfloat16


def layer_norm(values):
    center = values - jnp.mean(values, axis=-1, keepdims=True)
    spread = jnp.mean(center * center, axis=-1, keepdims=True)
    return center * lax.rsqrt(spread + 1e-06)


def is_grid(groups, experts):
    return groups == 2 and experts == 16


def chip_of(block):
    far = lax.axis_index("group") * 2
    mask = (block, block, block, block, 4 + far, 6 - far, 5 + far, 7 - far)[block]
    return jnp.bitwise_xor(lax.axis_index("expert") // 2, mask)


def core_of():
    return lax.axis_index("expert") % 2


def norm_kernel(tokens_ref, *refs):
    mine_ref, other_ref, scratch = refs[-3:]
    scratch[...] = layer_norm(tokens_ref[...].astype(F32)).astype(BF16)
    core = core_of()
    block = mine_ref.shape[1] // CHIPS
    for at in range(CHIPS):
        start = pl.multiple_of(chip_of(at) * block, block)
        columns = scratch[:, pl.ds(start, block)]
        swapped = pltpu.roll(columns.astype(F32), block // 2, 1).astype(BF16)
        place = slice(at * block, (at + 1) * block)
        mine_ref[:, place] = jnp.where(core == 0, columns, swapped)
        other_ref[:, place] = jnp.where(core == 0, swapped, columns)


def norm(tokens, image, length, before, others=(), cost=0):
    rows, width = tokens.shape
    piece = pl.BlockSpec((length, width), lambda step: (image, 0))
    return pl.pallas_call(
        norm_kernel,
        out_shape=[jax.ShapeDtypeStruct((rows, width), BF16)] * 2,
        grid=(1,),
        in_specs=[piece] + [pl.BlockSpec(memory_space=pl.ANY)] * len((*others, *before)),
        out_specs=[piece] * 2,
        scratch_shapes=[pltpu.VMEM((length, width), BF16)],
        input_output_aliases={1: 0, 2: 1} if others else {},
        compiler_params=pltpu.CompilerParams(vmem_limit_bytes=16 << 20),
        cost_estimate=pl.CostEstimate(
            flops=cost or 8 * length * width,
            bytes_accessed=6 * length * width,
            transcendentals=length,
        ),
        name="norm",
    )(tokens, *others, *before)


def copy_kernel(count, *refs):
    for source, target in zip(refs[:count], refs[-count:]):
        target[...] = source[...]


def copies(values, before):
    vmem = pl.BlockSpec(memory_space=pltpu.VMEM)
    return pl.pallas_call(
        functools.partial(copy_kernel, len(values)),
        out_shape=[jax.ShapeDtypeStruct(value.shape, value.dtype) for value in values],
        in_specs=[vmem] * len(values) + [pl.BlockSpec(memory_space=pl.ANY)] * len(before),
        out_specs=[vmem] * len(values),
        compiler_params=pltpu.CompilerParams(vmem_limit_bytes=4 << 20),
        cost_estimate=pl.CostEstimate(flops=0, bytes_accessed=0, transcendentals=0),
        name="copies",
    )(*values, *before)


def split_kernel(mine_ref, other_ref, *refs):
    span = mine_ref.shape[1] // 12
    rows = mine_ref.shape[0]
    for side, source in enumerate((mine_ref, other_ref)):
        for chunk in range(2):
            for which in range(3):
                start = (which * 4 + core_of() * 2 + chunk) * span
                refs[chunk - 2][
                    side * rows : (side + 1) * rows, which * span : (which + 1) * span
                ] = source[:, pl.ds(pl.multiple_of(start, span), span)]


def split_out_kernel(mine_ref, other_ref, *refs):
    span = mine_ref.shape[1] // 2
    rows = mine_ref.shape[0]
    for side, source in enumerate((mine_ref, other_ref)):
        start = pl.multiple_of(core_of() * span, span)
        refs[-1][side * rows : (side + 1) * rows] = source[:, pl.ds(start, span)]


def split(kernel, mine, other, count, columns, before=()):
    rows = mine.shape[0]
    vmem = pl.BlockSpec(memory_space=pltpu.VMEM)
    return pl.pallas_call(
        kernel,
        out_shape=[jax.ShapeDtypeStruct((2 * rows, columns), BF16)] * count,
        in_specs=[vmem] * 2 + [pl.BlockSpec(memory_space=pl.ANY)] * len(before),
        out_specs=[vmem] * count,
        compiler_params=pltpu.CompilerParams(vmem_limit_bytes=8 << 20),
        cost_estimate=pl.CostEstimate(
            flops=0, bytes_accessed=8 * rows * columns, transcendentals=0
        ),
        name="split",
    )(mine, other, *before)


def attend(query, keys, values, head, out_ref, rows, columns):
    lane = lax.broadcasted_iota(jnp.int32, query.shape, 1)
    first = lane < head
    result = []
    for mask in (first, ~first):
        scores = lax.dot_general(
            jnp.where(mask, query, jnp.zeros_like(query)),
            keys,
            (((1,), (1,)), ((), ())),
            preferred_element_type=F32,
        )
        top = jnp.max(scores, axis=-1, keepdims=True)
        weights = jnp.exp(scores - top).astype(BF16)
        mixed = jnp.dot(
            weights, jnp.where(mask, values, jnp.ones_like(values)), preferred_element_type=F32
        )
        result.append(mixed)
    sums = pltpu.roll(jnp.where(first, result[1], result[0]), head, 1)
    out_ref[rows, columns] = (jnp.where(first, result[0], result[1]) / sums).astype(BF16)


def attention_kernel(length, head, normed, weight, *refs):
    out_ref = refs[-1]
    span = out_ref.shape[1]
    pair = 2 * head

    def project(at):
        return jnp.dot(
            normed[...], weight[:, at * span : (at + 1) * span], preferred_element_type=F32
        )

    query = (project(0) * head**-0.5).astype(BF16)
    keys = project(1).astype(BF16)
    values = project(2).astype(BF16)
    for start in range(0, normed.shape[0], length):
        rows = slice(start, start + length)
        for left in range(0, span, pair):
            columns = slice(left, left + pair)
            attend(
                query[rows, columns],
                keys[rows, columns],
                values[rows, columns],
                head,
                out_ref,
                rows,
                columns,
            )


def attention(normed, weight, length, head, before=()):
    rows, width = normed.shape
    span = weight.shape[1] // 3
    vmem = pl.BlockSpec(memory_space=pltpu.VMEM)
    return pl.pallas_call(
        functools.partial(attention_kernel, length, head),
        out_shape=jax.ShapeDtypeStruct((rows, span), BF16),
        in_specs=[vmem] * 2 + [pl.BlockSpec(memory_space=pl.ANY)] * len(before),
        out_specs=vmem,
        compiler_params=pltpu.CompilerParams(vmem_limit_bytes=20 << 20),
        cost_estimate=pl.CostEstimate(
            flops=2 * rows * span * (3 * width + 2 * length),
            bytes_accessed=6 * width * span + 4 * rows * width,
            transcendentals=rows * (span // head) * length,
        ),
        name="attention",
    )(normed, weight, *before)


def router_kernel(count, images, length, *refs):
    tokens_ref, keys_ref = refs[:2]
    parts = refs[2:6]
    sources = refs[6:10]
    resid_ref, combine_ref, inputs_ref = refs[10:13]
    weight, sem = refs[13:]
    core = core_of()
    span = sources[0].shape[1]
    half = weight.shape[0] // (2 * count)
    copies = []
    for which, source in enumerate(sources):
        side = which // 2
        left = pl.multiple_of(jnp.bitwise_xor(core, side) * span, span)
        for at, block in enumerate((EARLY, LATE)[which % 2]):
            for part in range(2):
                start = (2 * chip_of(block) + jnp.bitwise_xor(core, part ^ side)) * half
                copy = pltpu.make_async_copy(
                    source.at[pl.ds((2 * at + part) * half, half)],
                    weight.at[pl.ds(pl.multiple_of(start, half), half), pl.ds(left, span)],
                    sem.at[len(copies)],
                )
                copy.start()
                copies.append(copy)
    for copy in copies:
        copy.wait()
    inner = parts[0].shape[1]
    for image in range(images):
        at = slice(image * length, (image + 1) * length)
        resid = tokens_ref[at].astype(F32)
        for which, part in enumerate(parts):
            side, chunk = which // 2, which % 2
            start = (2 * jnp.bitwise_xor(core, side) + chunk) * inner
            resid += jnp.dot(
                part[at],
                weight[pl.ds(pl.multiple_of(start, inner), inner)],
                preferred_element_type=F32,
            )
        resid_ref[at] = resid
        normed = layer_norm(resid).astype(BF16)
        logits = lax.dot_general(
            keys_ref[...], normed, (((1,), (1,)), ((), ())), preferred_element_type=F32
        )
        dispatch = jax.nn.softmax(logits, axis=1).astype(BF16)
        combine_ref[image] = jax.nn.softmax(logits, axis=0).astype(BF16)
        inputs_ref[image] = jnp.dot(dispatch, normed, preferred_element_type=F32).astype(BF16)


def router(tokens, slot_keys, parts, blocks, images, length):
    rows, width = tokens.shape
    slots = slot_keys.shape[1]
    count = CHIPS
    vmem = pl.BlockSpec(memory_space=pltpu.VMEM)
    hbm = pl.BlockSpec(memory_space=pl.ANY)
    return pl.pallas_call(
        functools.partial(router_kernel, count, images, length),
        out_shape=[
            jax.ShapeDtypeStruct((rows, width), F32),
            jax.ShapeDtypeStruct((images, slots, length), BF16),
            jax.ShapeDtypeStruct((images, slots, width), BF16),
        ],
        in_specs=[vmem] * 6 + [hbm] * 4,
        out_specs=[vmem] * 3,
        scratch_shapes=[
            pltpu.VMEM((width, width), BF16),
            pltpu.SemaphoreType.DMA((4 * count,)),
        ],
        compiler_params=pltpu.CompilerParams(vmem_limit_bytes=24 << 20),
        cost_estimate=pl.CostEstimate(
            flops=2 * rows * width * (width + 2 * slots),
            bytes_accessed=2 * width * width + 8 * rows * width,
            transcendentals=2 * rows * slots,
        ),
        name="router",
    )(tokens, slot_keys.T, *parts, *blocks)


def expert_kernel(inputs_ref, first_ref, second_ref, out_ref, total):
    step = pl.program_id(1)
    hidden = jnp.dot(inputs_ref[0], first_ref[0], preferred_element_type=F32)
    hidden = (0.5 * hidden * (1.0 + lax.erf(hidden * 0.5**0.5))).astype(BF16)
    answer = jnp.dot(hidden, second_ref[0], preferred_element_type=F32)

    @pl.when(step == 0)
    def _():
        total[...] = answer

    @pl.when(step > 0)
    def _():
        total[...] += answer

    @pl.when(step == pl.num_programs(1) - 1)
    def _():
        out_ref[0] = total[...].astype(BF16)


def experts_here(inputs, first, second):
    count, rows, width = inputs.shape
    hidden = first.shape[2]
    piece = hidden // EXPERT_STEPS
    return pl.pallas_call(
        expert_kernel,
        out_shape=jax.ShapeDtypeStruct(inputs.shape, BF16),
        grid=(count, EXPERT_STEPS),
        in_specs=[
            pl.BlockSpec((1, rows, width), lambda e, h: (e, 0, 0)),
            pl.BlockSpec((1, width, piece), lambda e, h: (e, 0, h)),
            pl.BlockSpec((1, piece, width), lambda e, h: (e, h, 0)),
        ],
        out_specs=pl.BlockSpec((1, rows, width), lambda e, h: (e, 0, 0)),
        scratch_shapes=[pltpu.VMEM((rows, width), F32)],
        compiler_params=pltpu.CompilerParams(vmem_limit_bytes=24 << 20),
        cost_estimate=pl.CostEstimate(
            flops=4 * count * rows * width * hidden,
            bytes_accessed=4 * count * width * hidden,
            transcendentals=count * rows * hidden,
        ),
        name="experts",
    )(inputs, first, second)


def front_on_grid(groups, experts, tokens, w_qkv, w_attn_out, slot_keys):
    images, length, width = tokens.shape
    head = width // HEADS
    flat = tokens.reshape(images * length, width)
    def send(value, move):
        pairs = []
        for at in range(groups):
            mask, flip = move(at)
            for index in range(experts):
                target = (at ^ flip) * experts + (index ^ mask)
                pairs.append((at * experts + index, target))
        return lax.ppermute(value, AXES, pairs)

    def in_chip(value):
        return send(value, lambda at: (1, 0))

    def over_y(value):
        return send(value, lambda at: (2, 0))

    def near_z(value):
        return send(value, lambda at: (4, 0))

    def far_z(value):
        return send(value, lambda at: (12, 0) if at else (8, 0))

    def over_x(value):
        return send(value, lambda at: (0, 1))

    span = width // 4
    a, b = split(split_kernel, w_qkv, in_chip(w_qkv), 2, 3 * span)

    def whole(*blocks):
        return jnp.concatenate(blocks, axis=0)

    def step(*values, done=()):
        nonlocal token
        *result, token = copies([*values, token], done)
        return result

    a_far = far_z(a)
    a_near = near_z(a)
    a_y = over_y(a)
    normed, normed_sent = norm(flat, 0, length, (a,), cost=LONG)
    token = normed[:8, :128]
    (b_1,) = step(b)
    b_y = over_y(b_1)
    a_far_1, b_2 = step(a_far, b, done=(a_y, a_near))
    b_far = far_z(b_2)
    a_x = over_x(a_far_1)
    a_y_far = over_y(a_far_1)
    (a_near_1,) = step(a_near, done=(b_y,))
    a_y_near = over_y(a_near_1)
    for image in range(1, images):
        normed, normed_sent = norm(flat, image, length, (token,), (normed, normed_sent), LONG)
    (a_y_far_1,) = step(a_y_far)
    a_x_far = over_x(a_y_far_1)
    (w_out,) = step(w_attn_out)
    (c,) = split(split_out_kernel, w_out, in_chip(w_out), 1, 2 * span)
    (b_3,) = step(b, done=(a_x,))
    b_near = near_z(b_3)
    normed_other = in_chip(normed_sent)
    b_far_1, c_2 = step(b_far, c, done=(a_y_near, a_x_far))
    b_x = over_x(b_far_1)
    b_y_far = over_y(b_far_1)
    c_far = far_z(c_2)
    a_all = whole(a, a_y, a_near, a_y_near, a_far, a_x, a_y_far, a_x_far)
    other_a = attention(normed_other, a_all, length, head, (token,))
    (b_near_1,) = step(b_near, done=(other_a,))
    b_y_near = over_y(b_near_1)
    (b_y_far_1,) = step(b_y_far)
    b_x_far = over_x(b_y_far_1)
    (c_3,) = step(c, done=(b_x,))
    c_near = near_z(c_3)
    c_y = over_y(c_3)
    (c_far_1,) = step(c_far)
    c_y_far = over_y(c_far_1)
    c_x = over_x(c_far_1)
    mine_a = attention(normed, a_all, length, head, (token,))
    (c_near_1,) = step(c_near, done=(b_y_near, mine_a))
    c_y_near = over_y(c_near_1)
    (c_y_far_1,) = step(c_y_far)
    c_x_far = over_x(c_y_far_1)
    (other_a_1,) = step(other_a, done=(b_x_far,))
    parts_a = in_chip(other_a_1)
    b_all = whole(b, b_y, b_near, b_y_near, b_far, b_x, b_y_far, b_x_far)
    other_b = attention(normed_other, b_all, length, head, (token,))
    early = whole(c, c_y, c_near, c_far, c_y_far)
    late = whole(c_y_near, c_x, c_x_far, jnp.concatenate([other_b[:16], other_b[16:32]], axis=1))
    parts_b = in_chip(other_b)
    mine_b = attention(normed, b_all, length, head, (other_b,))
    parts = [mine_a, mine_b, parts_a, parts_b]
    outs = [early, late, in_chip(early), in_chip(late)]
    return router(flat, slot_keys, parts, outs, images, length)


def front(tokens, w_qkv, w_attn_out, slot_keys):
    images, length, width = tokens.shape
    head = width // HEADS
    rows = images * length
    normed = layer_norm(tokens.astype(F32)).astype(BF16).reshape(rows, width)
    full_qkv = lax.all_gather(w_qkv, "expert", axis=0, tiled=True)
    qkv = jnp.dot(normed, full_qkv, preferred_element_type=F32).astype(BF16)
    query, keys, values = [
        part[:, :, 0] for part in jnp.split(qkv.reshape(images, length, 3, HEADS, head), 3, axis=2)
    ]
    scores = jnp.einsum("bqhd,bkhd->bhqk", query, keys, preferred_element_type=F32) * head**-0.5
    weights = jax.nn.softmax(scores, axis=-1).astype(BF16)
    attended = jnp.einsum("bhqk,bkhd->bqhd", weights, values, preferred_element_type=F32)
    full_out = lax.all_gather(w_attn_out, "expert", axis=0, tiled=True)
    projected = jnp.dot(
        attended.astype(BF16).reshape(rows, width), full_out, preferred_element_type=F32
    )
    resid = tokens.astype(F32).reshape(rows, width) + projected
    normed_two = layer_norm(resid).astype(BF16).reshape(images, length, width)
    logits = jnp.einsum("bsd,dn->bns", normed_two, slot_keys, preferred_element_type=F32)
    dispatch = jax.nn.softmax(logits, axis=2).astype(BF16)
    combine = jax.nn.softmax(logits, axis=1).astype(BF16)
    slot_inputs = jnp.einsum("bns,bsd->bnd", dispatch, normed_two, preferred_element_type=F32)
    return resid, combine, slot_inputs.astype(BF16)


def on_device(mesh_shape, tokens, w_qkv, w_attn_out, slot_keys, w_expert_in, w_expert_out):
    images, length, width = tokens.shape
    if is_grid(*mesh_shape):
        resid, combine, slot_inputs = front_on_grid(
            *mesh_shape, tokens, w_qkv, w_attn_out, slot_keys
        )
    else:
        resid, combine, slot_inputs = front(tokens, w_qkv, w_attn_out, slot_keys)
    slots = slot_keys.shape[1]
    sources = mesh_shape[1]
    expert_here = w_expert_in.shape[0]
    pairs = slots // (sources * expert_here)
    block = lax.all_to_all(slot_inputs, "expert", split_axis=1, concat_axis=1, tiled=True)
    arranged = block.reshape(images, sources, expert_here, pairs, width)
    arranged = arranged.transpose(2, 0, 1, 3, 4).reshape(expert_here, -1, width)
    answer = experts_here(arranged, w_expert_in, w_expert_out)
    answer = answer.reshape(expert_here, images, sources, pairs, width)
    answered = answer.transpose(1, 2, 0, 3, 4).reshape(images, slots, width)
    slot_outputs = lax.all_to_all(answered, "expert", split_axis=1, concat_axis=1, tiled=True)
    mixed = jnp.einsum("bns,bnd->bsd", combine, slot_outputs, preferred_element_type=F32)
    return (resid.reshape(images, length, width) + mixed).astype(BF16)


def solution(mesh):
    placed = (
        P(AXES, None, None),
        P("expert", None),
        P("expert", None),
        P(),
        P("expert", None, None),
        P("expert", None, None),
    )
    return jax.shard_map(
        functools.partial(on_device, (mesh.shape["group"], mesh.shape["expert"])),
        mesh=mesh,
        in_specs=placed,
        out_specs=P(AXES, None, None),
        check_vma=False,
    )
```
